128 devices in a mesh: rows: 32 (over y, x, core), cols: 4 (over z).
Axes of the slice: x: 4, y: 4, z: 4, core: 2. Of those that a mesh axis runs over, the one named last changes fastest.
Arguments:
- feats: bfloat16 [131072, 512], P('rows', 'cols'), may hold values from -6 to 6
- adj_vals: bfloat16 [1024, 16, 128, 128], P('rows'), may hold values from -0.125 to 0.125
- colref: int32 [1024, 16], P('rows'), may hold values from 0 to 95, as said below
- fetch_ids: int32 [32, 32, 2], P('rows'), may hold values from -1 to 31, as said below
- w_self: bfloat16 [512, 512], replicated, may hold values from -0.25 to 0.25
- w_neigh: bfloat16 [512, 512], replicated, may hold values from -0.25 to 0.25
- grad_out: bfloat16 [131072, 512], P(('rows', 'cols')), may hold values from -6 to 6
Outputs:
- act_out: bfloat16 [131072, 512], P(('rows', 'cols'))
- grad_self_w: float32 [512, 512], replicated
- grad_neigh_w: float32 [512, 512], replicated
- grad_feats: float32 [131072, 512], P('rows', 'cols')
The draws below stay inside these ranges and needn't reach their ends.
Inputs may be any that keep to these rules, and one draw needn't show every extreme that they name: `fetch_ids`: entry [r, o, s] is a row tile index within partition o (0 to 31) that partition r reads, or -1 for an empty slot. The entries of one r and o are distinct, all slots with o = r are empty, and every r fills all 2 slots of at least one o. `colref`: entry [b, k], with r = b // 32, is below 32 for partition r's own row tile of that index, or 32 + o * 2 + s for the slot s of fetch_ids[r, o], never an empty slot; so it lies in 0 to 32 + 32 * 2 - 1. The 16 entries of a row tile are distinct and the first is b - r * 32, the row tile itself.
All inputs are finite; a program needn't handle non-finite values.
Results may differ from the reference program's by a relative error of at most 0.0057.
Values may be sent and summed in bfloat16 or wider, within the bound.
A program may use at most 192 MiB of HBM per device.

```python
import math
import jax
import jax.numpy as jnp
from jax import lax

HID = 512
TILE = 128
RB = 32
K = 16
CAP = 2
NODES = 131072
NBLOCKS = 1024
N_ROWS = 32


def draw_plan(key):
    base = jax.random.fold_in(key, 11)
    key_live, key_full, key_pick, key_refs = jax.random.split(base, 4)
    partitions = N_ROWS
    reader = jnp.arange(partitions, dtype=jnp.int32)[:, None]
    owner_part = jnp.arange(partitions, dtype=jnp.int32)[None, :]
    live_count = jax.random.randint(key_live, (partitions, partitions), 1, CAP + 1, dtype=jnp.int32)
    full_pick = jax.random.randint(key_full, (partitions, 1), 0, partitions - 1, dtype=jnp.int32)
    full_owner = (reader + 1 + full_pick) % partitions
    live_count = jnp.where(owner_part == full_owner, CAP, live_count)
    live_count = jnp.where(owner_part == reader, 0, live_count)
    scores = jax.random.randint(key_pick, (partitions, partitions, RB), 0, 2 ** 20, dtype=jnp.int32) * RB + jnp.arange(RB, dtype=jnp.int32)
    ordering = jnp.argsort(scores, axis=-1, stable=True)[:, :, :CAP].astype(jnp.int32)
    slot_index = jnp.arange(CAP, dtype=jnp.int32)
    fetch_table = jnp.where(slot_index[None, None, :] < live_count[:, :, None], ordering, -1).astype(jnp.int32)
    pool_size = RB + partitions * CAP
    alive_slots = jnp.concatenate([jnp.ones((partitions, RB), jnp.int32), (fetch_table >= 0).astype(jnp.int32).reshape(partitions, partitions * CAP)], axis=1)
    ref_scores = jax.random.randint(key_refs, (partitions, RB, pool_size), 0, 2 ** 16, dtype=jnp.int32) * pool_size + jnp.arange(pool_size, dtype=jnp.int32)
    ref_scores = jnp.where(alive_slots[:, None, :] > 0, ref_scores, ref_scores + 2 ** 28)
    diagonal = jnp.arange(RB, dtype=jnp.int32)[:, None] == jnp.arange(pool_size, dtype=jnp.int32)[None, :]
    ref_scores = jnp.where(diagonal[None, :, :], -1, ref_scores)
    chosen = jnp.argsort(ref_scores, axis=-1, stable=True)[:, :, :K].astype(jnp.int32)
    return (fetch_table, chosen.reshape(partitions * RB, K))


def draw_colref(key, part):
    return draw_plan(key)[1]


def draw_fetch_ids(key, part):
    return draw_plan(key)[0]


def shard_levels(rng, extent, pieces, low, top_value):
    factor_of = 1.0
    for position, parts in pieces:
        steps = jax.random.uniform(jax.random.fold_in(jax.random.fold_in(rng, 6), position), (parts,), jnp.float32, low / len(pieces), top_value / len(pieces))
        factor_of = factor_of * jnp.repeat(jnp.exp(steps), extent[position] // parts).reshape((-1,) + (1,) * (len(extent) - 1 - position))
    return factor_of


def bell_draw(rng, dims, deviation, limit, cuts=(), kind=jnp.bfloat16):
    gain = shard_levels(rng, dims, cuts, -0.22, 0.18) if cuts else 1.0
    drawn = jax.random.normal(rng, dims, jnp.float32) * deviation * gain
    return jnp.minimum(jnp.maximum(drawn, -limit), limit).astype(kind)


def setup_inputs(seed: int = 0) -> dict:
    key_list = jax.random.split(jax.random.key(seed), 8)
    feats = bell_draw(key_list[0], (NODES, HID), 1.0, 6.0, ((0, 32), (1, 4)))
    adj_vals = bell_draw(key_list[1], (NBLOCKS, K, TILE, TILE), (K * TILE) ** -0.5, 0.125, ((0, 32),))
    colref = draw_colref(jax.random.fold_in(key_list[7], 71), 0)
    fetch_ids = draw_fetch_ids(jax.random.fold_in(key_list[7], 71), 0)
    w_self = bell_draw(key_list[4], (HID, HID), HID ** -0.5, 0.25)
    w_neigh = bell_draw(key_list[5], (HID, HID), HID ** -0.5, 0.25)
    grad_out = bell_draw(key_list[6], (NODES, HID), 1.0, 6.0, ((0, 128),))
    return {"feats": feats, "adj_vals": adj_vals, "colref": colref, "fetch_ids": fetch_ids, "w_self": w_self, "w_neigh": w_neigh, "grad_out": grad_out}


def tile_ids(colref, fetch_ids):
    count = colref.shape[0]
    reader = (jnp.arange(count, dtype=jnp.int32) // RB)[:, None]
    remote = jnp.maximum(colref - RB, 0).astype(jnp.int32)
    owner_part = remote // CAP
    slot_index = remote % CAP
    looked = fetch_ids[reader, owner_part, slot_index]
    return jnp.where(colref < RB, reader * RB + colref, owner_part * RB + looked).astype(jnp.int32)

def reference(feats, adj_vals, colref, fetch_ids, w_self, w_neigh, grad_out):
    all_tiles = feats.reshape(N_ROWS * RB, TILE, HID)
    tile_index = tile_ids(colref, fetch_ids).reshape(N_ROWS, RB, K)
    tile_vals = adj_vals.reshape(N_ROWS, RB, K, TILE, TILE)

    def aggregate(item_pair):
        index_set, values = item_pair
        picked = all_tiles[index_set]
        summed = jnp.einsum('bkij,bkjf->bif', values.astype(jnp.float32), picked.astype(jnp.float32))
        return summed.astype(jnp.bfloat16)
    aggregated = lax.map(aggregate, (tile_index, tile_vals)).reshape(NODES, HID)
    preact = jnp.dot(feats, w_self, preferred_element_type=jnp.float32) + jnp.dot(aggregated, w_neigh, preferred_element_type=jnp.float32)
    activation, pull_back = jax.vjp(jax.nn.gelu, preact)
    grad_pre = pull_back(grad_out.astype(jnp.float32))[0].astype(jnp.bfloat16)
    grad_scale = 1.0 / math.sqrt(NODES)
    contract = (((0,), (0,)), ((), ()))
    grad_self_w = lax.dot_general(feats, grad_pre, contract, preferred_element_type=jnp.float32) * grad_scale
    grad_neigh_w = lax.dot_general(aggregated, grad_pre, contract, preferred_element_type=jnp.float32) * grad_scale
    dims_back = (((1,), (1,)), ((), ()))
    self_part = lax.dot_general(grad_pre, w_self, dims_back, preferred_element_type=jnp.float32).astype(jnp.bfloat16)
    grad_agg = lax.dot_general(grad_pre, w_neigh, dims_back, preferred_element_type=jnp.float32).astype(jnp.bfloat16)
    grad_tiles = grad_agg.reshape(N_ROWS, RB, TILE, HID)

    def spread(running, item_set):
        index_set, values, grad_rows = item_set
        per_ref = jnp.einsum('bkij,bif->bkjf', values.astype(jnp.float32), grad_rows.astype(jnp.float32))
        pooled = jnp.zeros((N_ROWS * RB, TILE, HID), jnp.float32).at[index_set.reshape(-1)].add(per_ref.reshape(RB * K, TILE, HID))
        rounded = lax.optimization_barrier(pooled.astype(jnp.bfloat16))
        return (running + rounded.astype(jnp.float32), None)
    start_sum = jnp.zeros((N_ROWS * RB, TILE, HID), jnp.float32)
    summed_back, _ = lax.scan(spread, start_sum, (tile_index, tile_vals, grad_tiles))
    grad_feats = self_part.astype(jnp.float32) + summed_back.reshape(NODES, HID)
    return (activation.astype(jnp.bfloat16), grad_self_w, grad_neigh_w, grad_feats)
```

```python
import functools
import math

import jax
import jax.numpy as jnp
from jax import lax
from jax.experimental import pallas as pl
from jax.experimental.pallas import tpu as pltpu
from jax.sharding import PartitionSpec as P

MESH = pl.DeviceIdType.MESH
ANY = pl.BlockSpec(memory_space=pl.ANY)
VMEM = pl.BlockSpec(memory_space=pltpu.VMEM)
SMEM = pl.BlockSpec(memory_space=pltpu.SMEM)
BF16 = jnp.bfloat16
F32 = jnp.float32


def remote(src, dst, send, recv, axis, peer):
    return pltpu.make_async_remote_copy(
        src_ref=src, dst_ref=dst, send_sem=send, recv_sem=recv,
        device_id={axis: peer}, device_id_type=MESH,
    )


def forward_kernel(parts, cols, cap, blocks, per_block, fetch_ref, colref_ref, feats_hbm, adj_hbm,
                   frows_hbm, arows_hbm, wanted_ref,
                   pool, own_v, adj_v, stage, agg_v, idx_v, idx_s,
                   pool_sem, adj_sem, own_sem, ownv_sem, smem_sem,
                   idx_send, idx_recv, tile_send, tile_recv, f_send, f_recv, a_send, a_recv):
    me = lax.axis_index("rows")
    mc = lax.axis_index("cols")
    share = blocks // cols

    pltpu.make_async_copy(feats_hbm, own_v, ownv_sem).start()
    pltpu.make_async_copy(feats_hbm, pool.at[pl.ds(0, blocks)], pool_sem).start()
    for q in range(cols):
        pltpu.make_async_copy(adj_hbm.at[pl.ds(q * share, share)], adj_v.at[pl.ds(q * share, share)], adj_sem.at[q]).start()

    barrier = pltpu.get_barrier_semaphore()

    def hello(d, _):
        pl.semaphore_signal(barrier, inc=1, device_id={"rows": lax.rem(me + d, parts)}, device_id_type=MESH)
        return 0

    lax.fori_loop(1, parts, hello, 0)
    for d in range(1, cols):
        pl.semaphore_signal(barrier, inc=1, device_id={"cols": lax.rem(mc + d, cols)}, device_id_type=MESH)
    pl.semaphore_wait(barrier, parts - 1 + cols - 1)

    def ask(d, _):
        p = lax.rem(me + d, parts)
        remote(fetch_ref.at[p], idx_v.at[me], idx_send.at[p], idx_recv.at[me], "rows", p).start()
        return 0

    lax.fori_loop(1, parts, ask, 0)
    idx_v[me] = jnp.full(idx_v.shape[1:], -1, jnp.int32)

    for d in range(1, cols):
        p = lax.rem(mc + d, cols)
        remote(feats_hbm.at[pl.ds(p * share, share)], frows_hbm.at[mc], f_send.at[p], f_recv.at[mc], "cols", p).start()
    own = pltpu.make_async_copy(feats_hbm.at[pl.ds(mc * share, share)], frows_hbm.at[mc], own_sem)
    own.start()

    pltpu.make_async_copy(feats_hbm, own_v, ownv_sem).wait()

    def asked(d, _):
        p = lax.rem(me + parts - d, parts)
        remote(fetch_ref.at[p], idx_v.at[p], idx_send.at[p], idx_recv.at[p], "rows", p).wait_recv()
        return 0

    lax.fori_loop(1, parts, asked, 0)
    to_smem = pltpu.make_async_copy(idx_v, idx_s, smem_sem)
    to_smem.start()
    to_smem.wait()
    wanted_ref[...] = idx_v[...]

    def give(d, _):
        p = lax.rem(me + d, parts)
        for s in range(cap):
            stage[p, s] = own_v[jnp.maximum(idx_s[p, 0, s], 0)]
        remote(stage.at[p], pool.at[pl.ds(blocks + me * cap, cap)], tile_send.at[p], tile_recv.at[me], "rows", p).start()
        return 0

    lax.fori_loop(1, parts, give, 0)
    pool[pl.ds(blocks + me * cap, cap)] = jnp.zeros((cap,) + pool.shape[1:], BF16)
    pltpu.make_async_copy(feats_hbm, pool.at[pl.ds(0, blocks)], pool_sem).wait()
    for q in range(cols):
        pltpu.make_async_copy(adj_hbm.at[pl.ds(q * share, share)], adj_v.at[pl.ds(q * share, share)], adj_sem.at[q]).wait()

    def given(d, _):
        p = lax.rem(me + parts - d, parts)
        remote(stage.at[p], pool.at[pl.ds(blocks + p * cap, cap)], tile_send.at[p], tile_recv.at[p], "rows", p).wait_recv()
        return 0

    lax.fori_loop(1, parts, given, 0)

    def aggregate(b):
        left = jnp.concatenate([adj_v[b, k] for k in range(per_block)], axis=1)
        right = jnp.concatenate([pool[colref_ref[b * per_block + k]] for k in range(per_block)], axis=0)
        return jnp.dot(left, right, preferred_element_type=F32).astype(BF16)

    def tile_round(i, _):
        def one(d, _):
            p = lax.rem(mc + d, cols)
            agg_v[p, i] = aggregate(p * share + i)
            remote(agg_v.at[p, i], arows_hbm.at[mc, i], a_send.at[p, i], a_recv.at[mc, i], "cols", p).start()
            return 0

        lax.fori_loop(1, cols, one, 0)
        agg_v[mc, i] = aggregate(mc * share + i)
        return 0

    lax.fori_loop(0, share, tile_round, 0)
    own_agg = pltpu.make_async_copy(agg_v.at[mc], arows_hbm.at[mc], pool_sem)
    own_agg.start()

    for d in range(1, cols):
        p = lax.rem(mc + d, cols)
        remote(feats_hbm.at[pl.ds(p * share, share)], frows_hbm.at[p], f_send.at[p], f_recv.at[p], "cols", p).wait()
    own.wait()
    own_agg.wait()

    def drain(d, _):
        p = lax.rem(me + d, parts)
        remote(fetch_ref.at[p], idx_v.at[p], idx_send.at[p], idx_recv.at[p], "rows", p).wait_send()
        remote(stage.at[p], pool.at[pl.ds(blocks + p * cap, cap)], tile_send.at[p], tile_recv.at[p], "rows", p).wait_send()
        return 0

    lax.fori_loop(1, parts, drain, 0)

    def drain_agg(i, _):
        for d in range(1, cols):
            p = lax.rem(mc + d, cols)
            remote(agg_v.at[p, i], arows_hbm.at[p, i], a_send.at[p, i], a_recv.at[p, i], "cols", p).wait()
        return 0

    lax.fori_loop(0, share, drain_agg, 0)


def forward(fetch, colref, feats, adj, parts, cols, cap):
    blocks, per_block, tile, _ = adj.shape
    width = feats.shape[-1]
    share = blocks // cols
    DMA = pltpu.SemaphoreType.DMA
    rows_shape = jax.ShapeDtypeStruct((cols, share, tile, width), BF16)
    return pl.pallas_call(
        functools.partial(forward_kernel, parts, cols, cap, blocks, per_block),
        out_shape=(rows_shape, rows_shape, jax.ShapeDtypeStruct(fetch.shape, jnp.int32)),
        in_specs=[VMEM, SMEM, ANY, ANY],
        out_specs=(ANY, ANY, VMEM),
        scratch_shapes=[
            pltpu.VMEM((blocks + parts * cap, tile, width), BF16),
            pltpu.VMEM(feats.shape, BF16),
            pltpu.VMEM(adj.shape, BF16),
            pltpu.VMEM((parts, cap, tile, width), BF16),
            pltpu.VMEM((cols, share, tile, width), BF16),
            pltpu.VMEM(fetch.shape, jnp.int32),
            pltpu.SMEM(fetch.shape, jnp.int32),
            DMA, DMA((cols,)), DMA, DMA, DMA,
            DMA((parts,)), DMA((parts,)), DMA((parts,)), DMA((parts,)),
            DMA((cols,)), DMA((cols,)), DMA((cols, share)), DMA((cols, share)),
        ],
        compiler_params=pltpu.CompilerParams(collective_id=0, has_side_effects=True, vmem_limit_bytes=48 << 20),
        name="forward",
    )(fetch, colref, feats, adj)


def dense_kernel(scale, frows_ref, arows_ref, wself_ref, wneigh_ref, gout_ref,
                 act_ref, back_ref, gw_ref):
    cols, step, tile, width = frows_ref.shape
    hid = cols * width
    rows = step * tile
    step_id = pl.program_id(0)

    def rows_of(ref):
        return jnp.concatenate([ref[c].reshape(rows, width) for c in range(cols)], axis=1)

    both = jnp.concatenate([rows_of(frows_ref), rows_of(arows_ref)], axis=1)
    wself, wneigh = wself_ref[...], wneigh_ref[...]
    v = jnp.dot(both, jnp.concatenate([wself, wneigh], axis=0), preferred_element_type=F32)
    c0 = math.sqrt(2.0 / math.pi)
    v2 = v * v
    t = jnp.tanh(c0 * v * (1.0 + 0.044715 * v2))
    half = 0.5 * (1.0 + t)
    act_ref[...] = (v * half).astype(BF16)
    slope = half + (0.5 * v) * (1.0 - t * t) * (c0 * (1.0 + 3.0 * 0.044715 * v2))
    grad_pre = (gout_ref[...].astype(F32) * slope).astype(BF16)
    nt = (((1,), (1,)), ((), ()))
    for n, w in enumerate((wneigh, wself)):
        out = lax.dot_general(grad_pre, w, nt, preferred_element_type=F32).astype(BF16)
        for c in range(cols):
            back_ref[c, n] = out[:, c * width:(c + 1) * width].reshape(step, tile, width)
    gw = lax.dot_general(both, grad_pre, (((0,), (0,)), ((), ())), preferred_element_type=F32)

    @pl.when(step_id == 0)
    def _():
        gw_ref[...] = gw

    @pl.when(step_id > 0)
    def _():
        gw_ref[...] += gw

    @pl.when(step_id == pl.num_programs(0) - 1)
    def _():
        gw_ref[...] = gw_ref[...] * scale


def dense(frows, arows, wself, wneigh, gout, scale):
    cols, share, tile, width = frows.shape
    hid = cols * width
    step = 2
    block = pl.BlockSpec((cols, step, tile, width), lambda i: (0, i, 0, 0))
    whole = pl.BlockSpec((hid, hid), lambda i: (0, 0))
    rows = pl.BlockSpec((step * tile, hid), lambda i: (i, 0))
    return pl.pallas_call(
        functools.partial(dense_kernel, scale),
        grid=(share // step,),
        out_shape=(
            jax.ShapeDtypeStruct(gout.shape, BF16),
            jax.ShapeDtypeStruct((cols, 2, share, tile, width), BF16),
            jax.ShapeDtypeStruct((2 * hid, hid), F32),
        ),
        in_specs=[block, block, whole, whole, rows],
        out_specs=(
            rows,
            pl.BlockSpec((cols, 2, step, tile, width), lambda i: (0, 0, i, 0, 0)),
            pl.BlockSpec((2 * hid, hid), lambda i: (0, 0)),
        ),
        compiler_params=pltpu.CompilerParams(vmem_limit_bytes=48 << 20),
        name="dense",
    )(frows, arows, wself, wneigh, gout)


def spread_kernel(per_step, colref_ref, adj_ref, gagg_ref, own_ref, share_ref, pool):
    step_id = pl.program_id(0)
    blocks = own_ref.shape[0]
    per_block = adj_ref.shape[1]
    width = pool.shape[1]

    @pl.when(step_id == 0)
    def _():
        pool[...] = jnp.zeros_like(pool)

    for j in range(per_step):
        b = step_id * per_step + j
        grad_t = gagg_ref[j].T
        for k in range(0, per_block, 2):
            pair = jnp.concatenate([adj_ref[j, k], adj_ref[j, k + 1]], axis=1)
            out = jnp.dot(grad_t, pair, preferred_element_type=F32)
            half = out.shape[1] // 2
            pool[colref_ref[b * per_block + k]] += out[:, :half]
            pool[colref_ref[b * per_block + k + 1]] += out[:, half:]

    @pl.when(step_id == pl.num_programs(0) - 1)
    def _():
        def own(t, _):
            own_ref[t] = pool[t].astype(BF16).T
            return 0

        def away(t, _):
            share_ref[t] = pool[blocks + t].astype(BF16).T
            return 0

        lax.fori_loop(0, blocks, own, 0, unroll=4)
        lax.fori_loop(0, share_ref.shape[0], away, 0, unroll=4)


def spread(colref, adj, gagg, slots):
    blocks, per_block, tile, _ = adj.shape
    width = gagg.shape[-1]
    per_step = 4
    return pl.pallas_call(
        functools.partial(spread_kernel, per_step),
        grid=(blocks // per_step,),
        out_shape=(
            jax.ShapeDtypeStruct((blocks, tile, width), BF16),
            jax.ShapeDtypeStruct((slots, tile, width), BF16),
        ),
        in_specs=[
            SMEM,
            pl.BlockSpec((per_step, per_block, tile, tile), lambda i: (i, 0, 0, 0)),
            pl.BlockSpec((per_step, tile, width), lambda i: (i, 0, 0)),
        ],
        out_specs=(
            pl.BlockSpec((blocks, tile, width), lambda i: (0, 0, 0)),
            pl.BlockSpec((slots, tile, width), lambda i: (0, 0, 0)),
        ),
        scratch_shapes=[pltpu.VMEM((blocks + slots, width, tile), F32)],
        compiler_params=pltpu.CompilerParams(vmem_limit_bytes=48 << 20),
        name="spread",
    )(colref, adj, gagg)


def combine_kernel(wanted_ref, self_ref, own_ref, back_ref, out_ref):
    slots = back_ref.shape[0]
    out_ref[...] = self_ref[...].astype(F32) + own_ref[...].astype(F32)

    def add(s, _):
        t = wanted_ref[s]

        @pl.when(t >= 0)
        def _():
            out_ref[t] += back_ref[s].astype(F32)

        return 0

    lax.fori_loop(0, slots, add, 0)


def combine(wanted, self_part, own, back):
    return pl.pallas_call(
        combine_kernel,
        out_shape=jax.ShapeDtypeStruct(own.shape, F32),
        in_specs=[SMEM, VMEM, VMEM, VMEM],
        out_specs=VMEM,
        compiler_params=pltpu.CompilerParams(vmem_limit_bytes=48 << 20),
        name="combine",
    )(wanted, self_part, own, back)


def body(feats, adj_vals, colref, fetch_ids, w_self, w_neigh, grad_out):
    node_rows, width = feats.shape
    blocks, per_block, tile, _ = adj_vals.shape
    parts = lax.axis_size("rows")
    cols = lax.axis_size("cols")
    cap = fetch_ids.shape[2]
    slots = parts * cap
    hid = width * cols
    scale = 1.0 / math.sqrt(node_rows * parts)
    fetch = jnp.pad(fetch_ids.reshape(parts, 1, cap), ((0, 0), (0, 0), (0, 128 - cap)))
    refs = colref.reshape(blocks * per_block)
    frows, arows, wanted = forward(fetch, refs, feats.reshape(blocks, tile, width), adj_vals, parts, cols, cap)
    act, back, gw = dense(frows, arows, w_self, w_neigh, grad_out, scale)
    back = lax.all_to_all(back, "cols", split_axis=0, concat_axis=0, tiled=True)
    gagg = back[:, 0].reshape(blocks, tile, width)
    self_part = back[:, 1].reshape(blocks, tile, width)
    own, shares = spread(refs, adj_vals, gagg, slots)
    returned = lax.all_to_all(shares.reshape(parts, cap, tile, width), "rows", split_axis=0, concat_axis=0, tiled=True)
    pieces = lax.all_to_all(
        gw.astype(BF16).reshape(parts, 2 * hid // parts, hid), "rows", split_axis=0, concat_axis=0, tiled=True
    )
    piece = lax.psum(pieces.astype(F32).sum(axis=0), "cols")
    sums = lax.all_gather(piece, "rows", axis=0, tiled=True)
    grad_feats = combine(wanted[:, 0, :cap].reshape(slots), self_part, own, returned.reshape(slots, tile, width))
    return act, sums[:hid], sums[hid:], grad_feats.reshape(node_rows, width)


def solution(mesh):
    in_specs = (
        P("rows", "cols"),
        P("rows", None, None, None),
        P("rows", None),
        P("rows", None, None),
        P(),
        P(),
        P(("rows", "cols"), None),
    )
    out_specs = (P(("rows", "cols"), None), P(), P(), P("rows", "cols"))
    return jax.shard_map(body, mesh=mesh, in_specs=in_specs, out_specs=out_specs, check_vma=False)
```

```python
import functools
import math

import jax
import jax.numpy as jnp
from jax import lax
from jax.experimental import pallas as pl
from jax.experimental.pallas import tpu as pltpu
from jax.sharding import PartitionSpec as P

MESH = pl.DeviceIdType.MESH
ANY = pl.BlockSpec(memory_space=pl.ANY)
VMEM = pl.BlockSpec(memory_space=pltpu.VMEM)
SMEM = pl.BlockSpec(memory_space=pltpu.SMEM)
BF16 = jnp.bfloat16
F32 = jnp.float32


def remote(src, dst, send, recv, axis, peer):
    return pltpu.make_async_remote_copy(
        src_ref=src, dst_ref=dst, send_sem=send, recv_sem=recv,
        device_id={axis: peer}, device_id_type=MESH,
    )


def layer_kernel(parts, cols, cap, blocks, per_block, step, fetch_ref, colref_ref, feats_hbm, adj_hbm, w_self_hbm,
                 w_neigh_hbm, gout_hbm, act_ref, self_ref, gagg_hbm, w_ref, wanted_ref,
                 pool, own_v, adj_v, stage, agg_v, frows, arows, w_v, gout_v, gagg_v, gw, idx_v, idx_s,
                 pool_sem, adj_sem, own_sem, ownv_sem, w_sem, gout_sem, smem_sem,
                 idx_send, idx_recv, tile_send, tile_recv, f_send, f_recv, a_send, a_recv, g_send, g_recv):
    me = lax.axis_index("rows")
    mc = lax.axis_index("cols")
    share = blocks // cols
    groups = share // step
    tile, width = own_v.shape[1:]
    hid = cols * width

    local = [
        pltpu.make_async_copy(feats_hbm, own_v, ownv_sem),
        pltpu.make_async_copy(feats_hbm, pool.at[pl.ds(0, blocks)], pool_sem),
        pltpu.make_async_copy(feats_hbm.at[pl.ds(mc * share, share)], frows.at[mc], own_sem),
        pltpu.make_async_copy(w_self_hbm, w_v.at[pl.ds(0, hid)], w_sem.at[0]),
        pltpu.make_async_copy(w_neigh_hbm, w_v.at[pl.ds(hid, hid)], w_sem.at[1]),
        pltpu.make_async_copy(gout_hbm, gout_v, gout_sem),
    ]
    for q in range(cols):
        part = pl.ds(q * share, share)
        local.append(pltpu.make_async_copy(adj_hbm.at[part], adj_v.at[part], adj_sem.at[q]))
    local[0].start()

    barrier = pltpu.get_barrier_semaphore()

    def hello(d, _):
        pl.semaphore_signal(barrier, inc=1, device_id={"rows": lax.rem(me + d, parts)}, device_id_type=MESH)
        return 0

    lax.fori_loop(1, parts, hello, 0)
    for d in range(1, cols):
        pl.semaphore_signal(barrier, inc=1, device_id={"cols": lax.rem(mc + d, cols)}, device_id_type=MESH)
    pl.semaphore_wait(barrier, parts - 1 + cols - 1)

    def ask(d, _):
        p = lax.rem(me + d, parts)
        remote(fetch_ref.at[p], idx_v.at[me], idx_send.at[p], idx_recv.at[me], "rows", p).start()
        return 0

    lax.fori_loop(1, parts, ask, 0)
    idx_v[me] = jnp.full(idx_v.shape[1:], -1, jnp.int32)
    local[0].wait()

    def asked(d, _):
        p = lax.rem(me + parts - d, parts)
        remote(fetch_ref.at[p], idx_v.at[p], idx_send.at[p], idx_recv.at[p], "rows", p).wait_recv()
        return 0

    lax.fori_loop(1, parts, asked, 0)
    to_smem = pltpu.make_async_copy(idx_v, idx_s, smem_sem)
    to_smem.start()
    to_smem.wait()
    wanted_ref[...] = idx_v[...]

    def give(d, _):
        p = lax.rem(me + d, parts)
        for s in range(cap):
            stage[p, s] = own_v[jnp.maximum(idx_s[p, 0, s], 0)]
        remote(stage.at[p], pool.at[pl.ds(blocks + me * cap, cap)], tile_send.at[p], tile_recv.at[me], "rows", p).start()
        return 0

    lax.fori_loop(1, parts, give, 0)

    for d in range(1, cols):
        p = lax.rem(mc + d, cols)
        remote(own_v.at[pl.ds(p * share, share)], frows.at[mc], f_send.at[p], f_recv.at[mc], "cols", p).start()
    for copy in local[1:]:
        copy.start()
    pool[pl.ds(blocks + me * cap, cap)] = jnp.zeros((cap,) + pool.shape[1:], BF16)
    for copy in local[1:]:
        copy.wait()
    for d in range(1, cols):
        p = lax.rem(mc + d, cols)
        remote(own_v.at[pl.ds(p * share, share)], frows.at[p], f_send.at[p], f_recv.at[p], "cols", p).wait()

    def given(d, _):
        p = lax.rem(me + parts - d, parts)
        remote(stage.at[p], pool.at[pl.ds(blocks + p * cap, cap)], tile_send.at[p], tile_recv.at[p], "rows", p).wait_recv()
        return 0

    lax.fori_loop(1, parts, given, 0)

    def aggregate(b):
        left = jnp.concatenate([adj_v[b, k] for k in range(per_block)], axis=1)
        right = jnp.concatenate([pool[colref_ref[b * per_block + k]] for k in range(per_block)], axis=0)
        return jnp.dot(left, right, preferred_element_type=F32).astype(BF16)

    def agg_copy(p, slot, i):
        return remote(agg_v.at[p, i], arows.at[slot, i], a_send.at[p, i], a_recv.at[slot, i], "cols", p)

    def back_copy(p, slot, g):
        part = pl.ds(g * step, step)
        return remote(gagg_v.at[p, part], gagg_hbm.at[slot, part], g_send.at[p, g], g_recv.at[slot, g], "cols", p)

    def tile_round(i):
        def one(d, _):
            p = lax.rem(mc + d, cols)
            agg_v[p, i] = aggregate(p * share + i)
            agg_copy(p, mc, i).start()
            return 0

        lax.fori_loop(1, cols, one, 0)
        arows[mc, i] = aggregate(mc * share + i)

    def dense(g):
        part = pl.ds(g * step, step)
        for j in range(step):
            for d in range(1, cols):
                p = lax.rem(mc + d, cols)
                agg_copy(p, p, g * step + j).wait_recv()

        def rows_of(ref):
            return jnp.concatenate([ref[c, part].reshape(step * tile, width) for c in range(cols)], axis=1)

        both = jnp.concatenate([rows_of(frows), rows_of(arows)], axis=1)
        v = jnp.dot(both, w_v[...], preferred_element_type=F32)
        c0 = math.sqrt(2.0 / math.pi)
        v2 = v * v
        t = jnp.tanh(c0 * v * (1.0 + 0.044715 * v2))
        half = 0.5 * (1.0 + t)
        act_ref[part] = (v * half).astype(BF16).reshape(step, tile, hid)
        slope = half + (0.5 * v) * (1.0 - t * t) * (c0 * (1.0 + 3.0 * 0.044715 * v2))
        grad_pre = (gout_v[part].reshape(step * tile, hid).astype(F32) * slope).astype(BF16)
        nt = (((1,), (1,)), ((), ()))
        out = lax.dot_general(grad_pre, w_v[pl.ds(hid, hid)], nt, preferred_element_type=F32).astype(BF16)
        for c in range(cols):
            gagg_v[c, part] = out[:, c * width:(c + 1) * width].reshape(step, tile, width)
        for d in range(1, cols):
            back_copy(lax.rem(mc + d, cols), mc, g).start()
        out = lax.dot_general(grad_pre, w_v[pl.ds(0, hid)], nt, preferred_element_type=F32).astype(BF16)
        for c in range(cols):
            self_ref[c, part] = out[:, c * width:(c + 1) * width].reshape(step, tile, width)
        gw[...] += lax.dot_general(both, grad_pre, (((0,), (0,)), ((), ())), preferred_element_type=F32)

    gw[...] = jnp.zeros_like(gw)

    def work(g, _):
        @pl.when(g < groups)
        def _():
            for j in range(step):
                tile_round(g * step + j)

        @pl.when(g > 0)
        def _():
            dense(g - 1)

        return 0

    lax.fori_loop(0, groups + 1, work, 0)
    own_back = pltpu.make_async_copy(gagg_v.at[mc], gagg_hbm.at[mc], own_sem)
    own_back.start()

    halves, _, chips, rows_p, cols_p = w_ref.shape
    wide = hid // cols_p
    for n in range(halves * cols):
        for q in range(chips):
            at = n * (2 * hid // (halves * cols)) + (q // wide) * rows_p
            w_ref[n // cols, n % cols, q] = gw[at:at + rows_p, (q % wide) * cols_p:(q % wide + 1) * cols_p]

    own_back.wait()

    def drain(d, _):
        p = lax.rem(me + d, parts)
        remote(fetch_ref.at[p], idx_v.at[p], idx_send.at[p], idx_recv.at[p], "rows", p).wait_send()
        remote(stage.at[p], pool.at[pl.ds(blocks + p * cap, cap)], tile_send.at[p], tile_recv.at[p], "rows", p).wait_send()
        return 0

    lax.fori_loop(1, parts, drain, 0)

    def drain_agg(i, _):
        for d in range(1, cols):
            p = lax.rem(mc + d, cols)
            agg_copy(p, p, i).wait_send()
        return 0

    lax.fori_loop(0, share, drain_agg, 0)

    def drain_back(g, _):
        for d in range(1, cols):
            p = lax.rem(mc + d, cols)
            back_copy(p, p, g).wait()
        return 0

    lax.fori_loop(0, groups, drain_back, 0)


def layer(fetch, colref, feats, adj, w_self, w_neigh, gout, parts, cols, cap):
    blocks, per_block, tile, _ = adj.shape
    width = feats.shape[-1]
    share = blocks // cols
    hid = cols * width
    step = 2
    chips = parts // 2
    piece = (16, 2 * hid * hid // (2 * cols * chips * 16))
    DMA = pltpu.SemaphoreType.DMA
    rows_shape = (cols, share, tile, width)
    return pl.pallas_call(
        functools.partial(layer_kernel, parts, cols, cap, blocks, per_block, step),
        out_shape=(
            jax.ShapeDtypeStruct(gout.shape, BF16),
            jax.ShapeDtypeStruct(rows_shape, BF16),
            jax.ShapeDtypeStruct(rows_shape, BF16),
            jax.ShapeDtypeStruct((2, cols, chips) + piece, F32),
            jax.ShapeDtypeStruct(fetch.shape, jnp.int32),
        ),
        in_specs=[VMEM, SMEM, ANY, ANY, ANY, ANY, ANY],
        out_specs=(VMEM, VMEM, ANY, VMEM, VMEM),
        scratch_shapes=[
            pltpu.VMEM((blocks + parts * cap, tile, width), BF16),
            pltpu.VMEM(feats.shape, BF16),
            pltpu.VMEM(adj.shape, BF16),
            pltpu.VMEM((parts, cap, tile, width), BF16),
            pltpu.VMEM(rows_shape, BF16),
            pltpu.VMEM(rows_shape, BF16),
            pltpu.VMEM(rows_shape, BF16),
            pltpu.VMEM((2 * hid, hid), BF16),
            pltpu.VMEM(gout.shape, BF16),
            pltpu.VMEM(rows_shape, BF16),
            pltpu.VMEM((2 * hid, hid), F32),
            pltpu.VMEM(fetch.shape, jnp.int32),
            pltpu.SMEM(fetch.shape, jnp.int32),
            DMA, DMA((cols,)), DMA, DMA, DMA((2,)), DMA, DMA,
            DMA((parts,)), DMA((parts,)), DMA((parts,)), DMA((parts,)),
            DMA((cols,)), DMA((cols,)), DMA((cols, share)), DMA((cols, share)),
            DMA((cols, share // step)), DMA((cols, share // step)),
        ],
        compiler_params=pltpu.CompilerParams(collective_id=0, has_side_effects=True, vmem_limit_bytes=52 << 20),
        name="layer",
    )(fetch, colref, feats, adj, w_self, w_neigh, gout)


def spread_kernel(per_step, colref_ref, adj_ref, gagg_ref, own_ref, share_ref, pool):
    step_id = pl.program_id(0)
    blocks = own_ref.shape[0]
    per_block = adj_ref.shape[1]
    width = pool.shape[1]

    @pl.when(step_id == 0)
    def _():
        pool[...] = jnp.zeros_like(pool)

    for j in range(per_step):
        b = step_id * per_step + j
        grad_t = gagg_ref[j].T
        for k in range(0, per_block, 2):
            pair = jnp.concatenate([adj_ref[j, k], adj_ref[j, k + 1]], axis=1)
            out = jnp.dot(grad_t, pair, preferred_element_type=F32)
            half = out.shape[1] // 2
            pool[colref_ref[b * per_block + k]] += out[:, :half]
            pool[colref_ref[b * per_block + k + 1]] += out[:, half:]

    @pl.when(step_id == pl.num_programs(0) - 1)
    def _():
        def own(t, _):
            own_ref[t] = pool[t].astype(BF16).T
            return 0

        def away(t, _):
            share_ref[t] = pool[blocks + t].astype(BF16).T
            return 0

        lax.fori_loop(0, blocks, own, 0, unroll=4)
        lax.fori_loop(0, share_ref.shape[0], away, 0, unroll=4)


def spread(colref, adj, gagg, slots):
    blocks, per_block, tile, _ = adj.shape
    width = gagg.shape[-1]
    per_step = 4
    return pl.pallas_call(
        functools.partial(spread_kernel, per_step),
        grid=(blocks // per_step,),
        out_shape=(
            jax.ShapeDtypeStruct((blocks, tile, width), BF16),
            jax.ShapeDtypeStruct((slots, tile, width), BF16),
        ),
        in_specs=[
            SMEM,
            pl.BlockSpec((per_step, per_block, tile, tile), lambda i: (i, 0, 0, 0)),
            pl.BlockSpec((per_step, tile, width), lambda i: (i, 0, 0)),
        ],
        out_specs=(
            pl.BlockSpec((blocks, tile, width), lambda i: (0, 0, 0)),
            pl.BlockSpec((slots, tile, width), lambda i: (0, 0, 0)),
        ),
        scratch_shapes=[pltpu.VMEM((blocks + slots, width, tile), F32)],
        compiler_params=pltpu.CompilerParams(vmem_limit_bytes=48 << 20),
        name="spread",
    )(colref, adj, gagg)


def finish_kernel(parts, cols, share_hbm, self_hbm, w_ref, ret_hbm, selfp_hbm, sums_ref,
                  from_core, to_z, from_z, to_chip, from_chip, sums,
                  s_send, s_recv, p_send, p_recv, own_sem,
                  core_send, core_recv, z_send, z_recv, chip_send, chip_recv, up_send, up_recv):
    me = lax.axis_index("rows")
    mc = lax.axis_index("cols")
    core = lax.rem(me, 2)
    chip = me // 2
    chips = parts // 2
    mate = me + 1 - 2 * core

    barrier = pltpu.get_barrier_semaphore()

    def hello(d, _):
        pl.semaphore_signal(barrier, inc=1, device_id={"rows": lax.rem(me + d, parts)}, device_id_type=MESH)
        return 0

    lax.fori_loop(1, parts, hello, 0)
    for d in range(1, cols):
        pl.semaphore_signal(barrier, inc=1, device_id={"cols": lax.rem(mc + d, cols)}, device_id_type=MESH)
    pl.semaphore_wait(barrier, parts - 1 + cols - 1)

    def share_copy(p, slot):
        return remote(share_hbm.at[p], ret_hbm.at[slot], s_send.at[p], s_recv.at[slot], "rows", p)

    def shares(lo, hi):
        def one(d, _):
            share_copy(lax.rem(me + d, parts), me).start()
            return 0

        lax.fori_loop(lo, hi, one, 0)

    def self_copy(p, slot):
        return remote(self_hbm.at[p], selfp_hbm.at[slot], p_send.at[p], p_recv.at[slot], "cols", p)

    def others():
        return [lax.rem(mc + d, cols) for d in range(1, cols)]

    def over_chips(f):
        def one(d, _):
            f(lax.rem(chip + d, chips))
            return 0

        lax.fori_loop(1, chips, one, 0)

    pair = remote(w_ref.at[1 - core], from_core, core_send.at[0], core_recv.at[0], "rows", mate)
    pair.start()
    third = parts // 3
    shares(1, third)
    pair.wait()
    for c in range(cols):
        from_core[c] = from_core[c] + w_ref[core, c]
        to_z[c] = from_core[c].astype(BF16)

    def z_copy(p, slot):
        return remote(to_z.at[p], from_z.at[slot], z_send.at[0, p], z_recv.at[0, slot], "cols", p)

    for p in others():
        z_copy(p, mc).start()
    shares(third, 2 * third)
    for p in others():
        z_copy(p, p).wait()
    total = from_core[mc]
    for p in others():
        total = total + from_z[p].astype(F32)
    to_chip[...] = total.astype(BF16)

    def chip_copy(q, slot):
        return remote(to_chip.at[q], from_chip.at[slot], chip_send.at[q], chip_recv.at[slot], "rows", 2 * q + core)

    over_chips(lambda q: chip_copy(q, chip).start())
    shares(2 * third, parts)
    for p in others():
        self_copy(p, mc).start()
    own = pltpu.make_async_copy(self_hbm.at[mc], selfp_hbm.at[mc], own_sem)
    own.start()
    from_chip[chip] = to_chip[chip]
    over_chips(lambda q: chip_copy(q, q).wait())
    total = from_chip[0].astype(F32)
    for q in range(1, chips):
        total = total + from_chip[q].astype(F32)
    sums[core, mc, chip] = total.astype(BF16)

    def up_copy(q, slot):
        return remote(sums.at[core, mc, chip], sums.at[core, mc, slot], up_send.at[q], up_recv.at[slot], "rows", 2 * q + core)

    over_chips(lambda q: up_copy(q, chip).start())
    over_chips(lambda q: up_copy(q, q).wait())

    def z_up(p, slot):
        return remote(sums.at[core, mc], sums.at[core, slot], z_send.at[1, p], z_recv.at[1, slot], "cols", p)

    for p in others():
        z_up(p, mc).start()
    for p in others():
        z_up(p, p).wait()
    pair_up = remote(sums.at[core], sums.at[core], core_send.at[1], core_recv.at[1], "rows", mate)
    pair_up.start()
    pair_up.wait()
    sums_ref[...] = sums[...]

    for p in others():
        self_copy(p, p).wait()
    own.wait()

    def drain(d, _):
        p = lax.rem(me + d, parts)
        share_copy(p, p).wait()
        return 0

    lax.fori_loop(1, parts, drain, 0)


def finish(shares, self_rows, w):
    parts, cap, tile, width = shares.shape
    cols = self_rows.shape[0]
    chips = w.shape[2]
    piece = w.shape[3:]
    DMA = pltpu.SemaphoreType.DMA
    return pl.pallas_call(
        functools.partial(finish_kernel, parts, cols),
        out_shape=(
            jax.ShapeDtypeStruct(shares.shape, BF16),
            jax.ShapeDtypeStruct(self_rows.shape, BF16),
            jax.ShapeDtypeStruct(w.shape, BF16),
        ),
        in_specs=[ANY, ANY, VMEM],
        out_specs=(ANY, ANY, VMEM),
        scratch_shapes=[
            pltpu.VMEM((cols, chips) + piece, F32),
            pltpu.VMEM((cols, chips) + piece, BF16),
            pltpu.VMEM((cols, chips) + piece, BF16),
            pltpu.VMEM((chips,) + piece, BF16),
            pltpu.VMEM((chips,) + piece, BF16),
            pltpu.VMEM(w.shape, BF16),
            DMA((parts,)), DMA((parts,)), DMA((cols,)), DMA((cols,)), DMA,
            DMA((2,)), DMA((2,)), DMA((2, cols)), DMA((2, cols)),
            DMA((chips,)), DMA((chips,)), DMA((chips,)), DMA((chips,)),
        ],
        compiler_params=pltpu.CompilerParams(collective_id=1, has_side_effects=True, vmem_limit_bytes=40 << 20),
        name="finish",
    )(shares, self_rows, w)


def combine_kernel(scale, wanted_ref, self_ref, own_ref, back_ref, sums_ref, out_ref, gs_ref, gn_ref):
    slots = back_ref.shape[0]
    out_ref[...] = self_ref[...].astype(F32) + own_ref[...].astype(F32)

    def add(s, _):
        t = wanted_ref[s]

        @pl.when(t >= 0)
        def _():
            out_ref[t] += back_ref[s].astype(F32)

        return 0

    lax.fori_loop(0, slots, add, 0)
    halves, cols, chips, rows_p, cols_p = sums_ref.shape
    hid = gs_ref.shape[0]
    wide = hid // cols_p
    for half, ref in enumerate((gs_ref, gn_ref)):
        for c in range(cols):
            for q in range(chips):
                at = c * (hid // cols) + (q // wide) * rows_p
                ref[at:at + rows_p, (q % wide) * cols_p:(q % wide + 1) * cols_p] = sums_ref[half, c, q].astype(F32) * scale


def combine(wanted, self_part, own, back, sums, scale):
    hid = own.shape[-1] * sums.shape[1]
    weights = jax.ShapeDtypeStruct((hid, hid), F32)
    return pl.pallas_call(
        functools.partial(combine_kernel, scale),
        out_shape=(jax.ShapeDtypeStruct(own.shape, F32), weights, weights),
        in_specs=[SMEM, VMEM, VMEM, VMEM, VMEM],
        out_specs=(VMEM, VMEM, VMEM),
        compiler_params=pltpu.CompilerParams(vmem_limit_bytes=40 << 20),
        name="combine",
    )(wanted, self_part, own, back, sums)


def body(feats, adj_vals, colref, fetch_ids, w_self, w_neigh, grad_out):
    node_rows, width = feats.shape
    blocks, per_block, tile, _ = adj_vals.shape
    parts = lax.axis_size("rows")
    cols = lax.axis_size("cols")
    cap = fetch_ids.shape[2]
    slots = parts * cap
    hid = width * cols
    scale = 1.0 / math.sqrt(node_rows * parts)
    fetch = jnp.pad(fetch_ids.reshape(parts, 1, cap), ((0, 0), (0, 0), (0, 128 - cap)))
    refs = colref.reshape(blocks * per_block)
    gout = grad_out.reshape(blocks // cols, tile, hid)
    act, self_rows, gagg, w, wanted = layer(
        fetch, refs, feats.reshape(blocks, tile, width), adj_vals, w_self, w_neigh, gout, parts, cols, cap
    )
    own, shares = spread(refs, adj_vals, gagg.reshape(blocks, tile, width), slots)
    returned, self_part, sums = finish(shares.reshape(parts, cap, tile, width), self_rows, w)
    grad_feats, grad_self, grad_neigh = combine(
        wanted[:, 0, :cap].reshape(slots), self_part.reshape(blocks, tile, width), own,
        returned.reshape(slots, tile, width), sums, scale,
    )
    return act.reshape(grad_out.shape), grad_self, grad_neigh, grad_feats.reshape(node_rows, width)


def solution(mesh):
    in_specs = (
        P("rows", "cols"),
        P("rows", None, None, None),
        P("rows", None),
        P("rows", None, None),
        P(),
        P(),
        P(("rows", "cols"), None),
    )
    out_specs = (P(("rows", "cols"), None), P(), P(), P("rows", "cols"))
    return jax.shard_map(body, mesh=mesh, in_specs=in_specs, out_specs=out_specs, check_vma=False)
```

```python
import functools
import math

import jax
import jax.numpy as jnp
from jax import lax
from jax.experimental import pallas as pl
from jax.experimental.pallas import tpu as pltpu
from jax.sharding import PartitionSpec as P

MESH = pl.DeviceIdType.MESH
ANY = pl.BlockSpec(memory_space=pl.ANY)
VMEM = pl.BlockSpec(memory_space=pltpu.VMEM)
SMEM = pl.BlockSpec(memory_space=pltpu.SMEM)
BF16 = jnp.bfloat16
F32 = jnp.float32


def remote(src, dst, send, recv, axis, peer):
    return pltpu.make_async_remote_copy(
        src_ref=src, dst_ref=dst, send_sem=send, recv_sem=recv,
        device_id={axis: peer}, device_id_type=MESH,
    )


def send_order(parts):
    side = math.isqrt(parts // 2)
    hops = lambda n: min(n, side - n)
    offsets = [(y, x, c) for y in range(side) for x in range(side) for c in range(2)][1:]
    return sorted(offsets, key=lambda o: (-hops(o[0]) - hops(o[1]), o[2]))


def at_offset(me, parts, offset):
    side = math.isqrt(parts // 2)
    dy, dx, dc = offset
    core, chip = lax.rem(me, 2), me // 2
    y, x = lax.rem(chip // side + dy, side), lax.rem(lax.rem(chip, side) + dx, side)
    return (y * side + x) * 2 + (1 - core if dc else core)


def layer_kernel(parts, cols, cap, blocks, per_block, step, fetch_ref, colref_ref, feats_hbm, adj_hbm, w_self_hbm,
                 w_neigh_hbm, gout_hbm, act_ref, self_ref, gagg_hbm, w_own_ref, w_send_refs, wanted_ref,
                 pool, own_v, adj_v, stage, agg_v, frows, arows, w_v, gout_v, gagg_v, gw, from_core, w_half, idx_v, idx_s,
                 pool_sem, adj_sem, own_sem, ownv_sem, w_sem, gout_sem, smem_sem,
                 idx_send, idx_recv, tile_send, tile_recv, f_send, f_recv, a_send, a_recv, g_send, g_recv,
                 core_send, core_recv):
    me = lax.axis_index("rows")
    mc = lax.axis_index("cols")
    share = blocks // cols
    groups = share // step
    tile, width = own_v.shape[1:]
    hid = cols * width

    local = [
        pltpu.make_async_copy(feats_hbm, own_v, ownv_sem),
        pltpu.make_async_copy(feats_hbm, pool.at[pl.ds(0, blocks)], pool_sem),
        pltpu.make_async_copy(feats_hbm.at[pl.ds(mc * share, share)], frows.at[mc], own_sem),
        pltpu.make_async_copy(w_self_hbm, w_v.at[pl.ds(0, hid)], w_sem.at[0]),
        pltpu.make_async_copy(w_neigh_hbm, w_v.at[pl.ds(hid, hid)], w_sem.at[1]),
        pltpu.make_async_copy(gout_hbm, gout_v, gout_sem),
    ]
    for q in range(cols):
        part = pl.ds(q * share, share)
        local.append(pltpu.make_async_copy(adj_hbm.at[part], adj_v.at[part], adj_sem.at[q]))
    local[0].start()

    barrier = pltpu.get_barrier_semaphore()

    def hello(d, _):
        pl.semaphore_signal(barrier, inc=1, device_id={"rows": lax.rem(me + d, parts)}, device_id_type=MESH)
        return 0

    lax.fori_loop(1, parts, hello, 0)
    for d in range(1, cols):
        pl.semaphore_signal(barrier, inc=1, device_id={"cols": lax.rem(mc + d, cols)}, device_id_type=MESH)
    pl.semaphore_wait(barrier, parts - 1 + cols - 1)

    def ask(d, _):
        p = lax.rem(me + d, parts)
        remote(fetch_ref, idx_v.at[me], idx_send.at[p], idx_recv.at[me], "rows", p).start()
        return 0

    lax.fori_loop(1, parts, ask, 0)
    idx_v[me] = jnp.full(idx_v.shape[1:], -1, jnp.int32)
    local[0].wait()

    def asked(d, _):
        p = lax.rem(me + parts - d, parts)
        remote(fetch_ref, idx_v.at[p], idx_send.at[p], idx_recv.at[p], "rows", p).wait_recv()
        return 0

    lax.fori_loop(1, parts, asked, 0)
    to_smem = pltpu.make_async_copy(idx_v, idx_s, smem_sem)
    to_smem.start()
    to_smem.wait()
    for offset in send_order(parts):
        p = at_offset(me, parts, offset)
        for s in range(cap):
            stage[p, s] = own_v[jnp.maximum(idx_s[p, s, me], 0)]
        remote(stage.at[p], pool.at[pl.ds(blocks + me * cap, cap)], tile_send.at[p], tile_recv.at[me], "rows", p).start()

    for d in range(1, cols):
        p = lax.rem(mc + d, cols)
        remote(own_v.at[pl.ds(p * share, share)], frows.at[mc], f_send.at[p], f_recv.at[mc], "cols", p).start()
    for copy in local[1:]:
        copy.start()

    def want(p, _):
        for s in range(cap):
            wanted_ref[p * cap + s] = idx_s[p, s, me]
        return 0

    lax.fori_loop(0, parts, want, 0)
    pool[pl.ds(blocks + me * cap, cap)] = jnp.zeros((cap,) + pool.shape[1:], BF16)
    for copy in local[1:]:
        copy.wait()
    for d in range(1, cols):
        p = lax.rem(mc + d, cols)
        remote(own_v.at[pl.ds(p * share, share)], frows.at[p], f_send.at[p], f_recv.at[p], "cols", p).wait()

    def given(d, _):
        p = lax.rem(me + parts - d, parts)
        remote(stage.at[p], pool.at[pl.ds(blocks + p * cap, cap)], tile_send.at[p], tile_recv.at[p], "rows", p).wait_recv()
        return 0

    lax.fori_loop(1, parts, given, 0)

    def aggregate(b):
        left = jnp.concatenate([adj_v[b, k] for k in range(per_block)], axis=1)
        right = jnp.concatenate([pool[colref_ref[k, b]] for k in range(per_block)], axis=0)
        return jnp.dot(left, right, preferred_element_type=F32).astype(BF16)

    def agg_copy(p, slot, i):
        return remote(agg_v.at[p, i], arows.at[slot, i], a_send.at[p, i], a_recv.at[slot, i], "cols", p)

    def back_copy(p, slot, g):
        part = pl.ds(g * step, step)
        return remote(gagg_v.at[p, part], gagg_hbm.at[slot, part], g_send.at[p, g], g_recv.at[slot, g], "cols", p)

    def tile_round(i):
        def one(d, _):
            p = lax.rem(mc + d, cols)
            agg_v[p, i] = aggregate(p * share + i)
            agg_copy(p, mc, i).start()
            return 0

        lax.fori_loop(1, cols, one, 0)
        arows[mc, i] = aggregate(mc * share + i)

    def dense(g):
        part = pl.ds(g * step, step)
        for j in range(step):
            for d in range(1, cols):
                p = lax.rem(mc + d, cols)
                agg_copy(p, p, g * step + j).wait_recv()

        def rows_of(ref):
            return jnp.concatenate([ref[c, part].reshape(step * tile, width) for c in range(cols)], axis=1)

        both = jnp.concatenate([rows_of(frows), rows_of(arows)], axis=1)
        v = jnp.dot(both, w_v[...], preferred_element_type=F32)
        c0 = math.sqrt(2.0 / math.pi)
        v2 = v * v
        t = jnp.tanh(c0 * v * (1.0 + 0.044715 * v2))
        half = 0.5 * (1.0 + t)
        act_ref[part] = (v * half).astype(BF16).reshape(step, tile, hid)
        slope = half + (0.5 * v) * (1.0 - t * t) * (c0 * (1.0 + 3.0 * 0.044715 * v2))
        grad_pre = (gout_v[part].reshape(step * tile, hid).astype(F32) * slope).astype(BF16)
        nt = (((1,), (1,)), ((), ()))
        out = lax.dot_general(grad_pre, w_v[pl.ds(hid, hid)], nt, preferred_element_type=F32).astype(BF16)
        for c in range(cols):
            gagg_v[c, part] = out[:, c * width:(c + 1) * width].reshape(step, tile, width)
        for d in range(1, cols):
            back_copy(lax.rem(mc + d, cols), mc, g).start()
        out = lax.dot_general(grad_pre, w_v[pl.ds(0, hid)], nt, preferred_element_type=F32).astype(BF16)
        for c in range(cols):
            self_ref[c, part] = out[:, c * width:(c + 1) * width].reshape(step, tile, width)
        sums = lax.dot_general(both, grad_pre, (((0,), (0,)), ((), ())), preferred_element_type=F32)
        gw[...] += sums.reshape(gw.shape)

    gw[...] = jnp.zeros_like(gw)

    def work(g, _):
        @pl.when(g < groups)
        def _():
            for j in range(step):
                tile_round(g * step + j)

        @pl.when(g > 0)
        def _():
            dense(g - 1)

        return 0

    lax.fori_loop(0, groups + 1, work, 0)
    own_back = pltpu.make_async_copy(gagg_v.at[mc], gagg_hbm.at[mc], own_sem)
    own_back.start()

    core = lax.rem(me, 2)
    mate = me + 1 - 2 * core
    pair = remote(gw.at[1 - core], from_core, core_send, core_recv, "rows", mate)
    pair.start()
    pair.wait()
    _, chips, rows_p, cols_p = w_half.shape
    wide = hid // cols_p
    for c in range(cols):
        for q in range(chips):
            down = pl.ds(c * (hid // cols) + (q // wide) * rows_p, rows_p)
            across = pl.ds((q % wide) * cols_p, cols_p)
            w_half[c, q] = gw[core, down, across] + from_core[down, across]
    w_own_ref[...] = w_half[mc]
    for d in range(1, cols):
        w_send_refs[d - 1][...] = w_half[lax.rem(mc + d, cols)].astype(BF16)

    own_back.wait()

    def drain(d, _):
        p = lax.rem(me + d, parts)
        remote(fetch_ref, idx_v.at[p], idx_send.at[p], idx_recv.at[p], "rows", p).wait_send()
        remote(stage.at[p], pool.at[pl.ds(blocks + p * cap, cap)], tile_send.at[p], tile_recv.at[p], "rows", p).wait_send()
        return 0

    lax.fori_loop(1, parts, drain, 0)

    def drain_agg(i, _):
        for d in range(1, cols):
            p = lax.rem(mc + d, cols)
            agg_copy(p, p, i).wait_send()
        return 0

    lax.fori_loop(0, share, drain_agg, 0)

    def drain_back(g, _):
        for d in range(1, cols):
            p = lax.rem(mc + d, cols)
            back_copy(p, p, g).wait()
        return 0

    lax.fori_loop(0, groups, drain_back, 0)


def layer(fetch, colref, feats, adj, w_self, w_neigh, gout, parts, cols, cap):
    blocks, per_block, tile, _ = adj.shape
    width = feats.shape[-1]
    share = blocks // cols
    hid = cols * width
    step = 2
    chips = parts // 2
    piece = (16, 2 * hid * hid // (2 * cols * chips * 16))
    DMA = pltpu.SemaphoreType.DMA
    rows_shape = (cols, share, tile, width)
    return pl.pallas_call(
        functools.partial(layer_kernel, parts, cols, cap, blocks, per_block, step),
        out_shape=(
            jax.ShapeDtypeStruct(gout.shape, BF16),
            jax.ShapeDtypeStruct(rows_shape, BF16),
            jax.ShapeDtypeStruct(rows_shape, BF16),
            jax.ShapeDtypeStruct((chips,) + piece, F32),
            (jax.ShapeDtypeStruct((chips,) + piece, BF16),) * (cols - 1),
            jax.ShapeDtypeStruct((parts * cap,), jnp.int32),
        ),
        in_specs=[VMEM, SMEM, ANY, ANY, ANY, ANY, ANY],
        out_specs=(VMEM, VMEM, ANY, VMEM, (VMEM,) * (cols - 1), SMEM),
        scratch_shapes=[
            pltpu.VMEM((blocks + parts * cap, tile, width), BF16),
            pltpu.VMEM(feats.shape, BF16),
            pltpu.VMEM(adj.shape, BF16),
            pltpu.VMEM((parts, cap, tile, width), BF16),
            pltpu.VMEM(rows_shape, BF16),
            pltpu.VMEM(rows_shape, BF16),
            pltpu.VMEM(rows_shape, BF16),
            pltpu.VMEM((2 * hid, hid), BF16),
            pltpu.VMEM(gout.shape, BF16),
            pltpu.VMEM(rows_shape, BF16),
            pltpu.VMEM((2, hid, hid), F32),
            pltpu.VMEM((hid, hid), F32),
            pltpu.VMEM((cols, chips) + piece, F32),
            pltpu.VMEM((parts,) + fetch.shape, jnp.int32),
            pltpu.SMEM((parts,) + fetch.shape, jnp.int32),
            DMA, DMA((cols,)), DMA, DMA, DMA((2,)), DMA, DMA,
            DMA((parts,)), DMA((parts,)), DMA((parts,)), DMA((parts,)),
            DMA((cols,)), DMA((cols,)), DMA((cols, share)), DMA((cols, share)),
            DMA((cols, share // step)), DMA((cols, share // step)), DMA, DMA,
        ],
        compiler_params=pltpu.CompilerParams(collective_id=0, has_side_effects=True, vmem_limit_bytes=62 << 20),
        name="layer",
    )(fetch, colref, feats, adj, w_self, w_neigh, gout)


def spread_kernel(per_step, colref_ref, adj_ref, gagg_ref, act_ref, own_ref, share_ref, act_out_ref, pool):
    step_id = pl.program_id(0)
    blocks = own_ref.shape[0]
    per_block = adj_ref.shape[1]
    width = pool.shape[1]

    act_out_ref[...] = act_ref[...]

    @pl.when(step_id == 0)
    def _():
        pool[...] = jnp.zeros_like(pool)

    for j in range(per_step):
        b = step_id * per_step + j
        grad_t = gagg_ref[j].T
        for k in range(0, per_block, 2):
            pair = jnp.concatenate([adj_ref[j, k], adj_ref[j, k + 1]], axis=1)
            out = jnp.dot(grad_t, pair, preferred_element_type=F32)
            half = out.shape[1] // 2
            pool[colref_ref[k, b]] += out[:, :half]
            pool[colref_ref[k + 1, b]] += out[:, half:]

    @pl.when(step_id == pl.num_programs(0) - 1)
    def _():
        def own(t, _):
            own_ref[t] = pool[t].astype(BF16).T
            return 0

        def away(t, _):
            share_ref[t] = pool[blocks + t].astype(BF16).T
            return 0

        lax.fori_loop(0, blocks, own, 0, unroll=4)
        lax.fori_loop(0, share_ref.shape[0], away, 0, unroll=4)


def spread(colref, adj, gagg, act, slots):
    blocks, per_block, tile, _ = adj.shape
    width = gagg.shape[-1]
    per_step = 4
    return pl.pallas_call(
        functools.partial(spread_kernel, per_step),
        grid=(blocks // per_step,),
        out_shape=(
            jax.ShapeDtypeStruct((blocks, tile, width), BF16),
            jax.ShapeDtypeStruct((slots, tile, width), BF16),
            jax.ShapeDtypeStruct(act.shape, BF16),
        ),
        in_specs=[
            SMEM,
            pl.BlockSpec((per_step, per_block, tile, tile), lambda i: (i, 0, 0, 0)),
            pl.BlockSpec((per_step, tile, width), lambda i: (i, 0, 0)),
            pl.BlockSpec((act.shape[0] * per_step // blocks,) + act.shape[1:], lambda i: (i, 0, 0)),
        ],
        out_specs=(
            pl.BlockSpec((blocks, tile, width), lambda i: (0, 0, 0)),
            pl.BlockSpec((slots, tile, width), lambda i: (0, 0, 0)),
            pl.BlockSpec((act.shape[0] * per_step // blocks,) + act.shape[1:], lambda i: (i, 0, 0)),
        ),
        scratch_shapes=[pltpu.VMEM((blocks + slots, width, tile), F32)],
        compiler_params=pltpu.CompilerParams(vmem_limit_bytes=48 << 20),
        cost_estimate=pl.CostEstimate(flops=2 * adj.size * width, bytes_accessed=2 * adj.size, transcendentals=0),
        name="spread",
    )(colref, adj, gagg, act)


def finish_kernel(parts, cols, share_hbm, self_hbm, w_own_ref, w_refs, ret_hbm, selfp_hbm, sums_ref,
                  to_chip, from_chip, sums,
                  s_send, s_recv, p_send, p_recv, own_sem,
                  core_send, core_recv, z_send, z_recv, chip_send, chip_recv, up_send, up_recv):
    me = lax.axis_index("rows")
    mc = lax.axis_index("cols")
    core = lax.rem(me, 2)
    chip = me // 2
    chips = parts // 2
    mate = me + 1 - 2 * core

    barrier = pltpu.get_barrier_semaphore()

    def hello(d, _):
        pl.semaphore_signal(barrier, inc=1, device_id={"rows": lax.rem(me + d, parts)}, device_id_type=MESH)
        return 0

    lax.fori_loop(1, parts, hello, 0)
    for d in range(1, cols):
        pl.semaphore_signal(barrier, inc=1, device_id={"cols": lax.rem(mc + d, cols)}, device_id_type=MESH)
    pl.semaphore_wait(barrier, parts - 1 + cols - 1)

    def share_copy(p, slot):
        return remote(share_hbm.at[p], ret_hbm.at[slot], s_send.at[p], s_recv.at[slot], "rows", p)

    order = send_order(parts)

    def shares(lo, hi):
        for offset in order[lo:hi]:
            share_copy(at_offset(me, parts, offset), me).start()

    def self_copy(p, slot):
        return remote(self_hbm.at[p], selfp_hbm.at[slot], p_send.at[p], p_recv.at[slot], "cols", p)

    def others():
        return [lax.rem(mc + d, cols) for d in range(1, cols)]

    def over_chips(f):
        def one(d, _):
            f(lax.rem(chip + d, chips))
            return 0

        lax.fori_loop(1, chips, one, 0)

    total = w_own_ref[...]
    for ref in w_refs:
        total = total + ref[...].astype(F32)
    to_chip[...] = total.astype(BF16)

    def chip_copy(q, slot):
        return remote(to_chip.at[q], from_chip.at[slot], chip_send.at[q], chip_recv.at[slot], "rows", 2 * q + core)

    over_chips(lambda q: chip_copy(q, chip).start())
    for p in others():
        self_copy(p, mc).start()
    shares(0, 8)
    own = pltpu.make_async_copy(self_hbm.at[mc], selfp_hbm.at[mc], own_sem)
    own.start()
    from_chip[chip] = to_chip[chip]
    over_chips(lambda q: chip_copy(q, q).wait())
    total = from_chip[0].astype(F32)
    for q in range(1, chips):
        total = total + from_chip[q].astype(F32)
    sums[core, mc, chip] = total.astype(BF16)

    def up_copy(q, slot):
        return remote(sums.at[core, mc, chip], sums.at[core, mc, slot], up_send.at[q], up_recv.at[slot], "rows", 2 * q + core)

    over_chips(lambda q: up_copy(q, chip).start())
    shares(8, 18)
    over_chips(lambda q: up_copy(q, q).wait())

    def z_up(p, slot):
        return remote(sums.at[core, mc], sums.at[core, slot], z_send.at[p], z_recv.at[slot], "cols", p)

    for p in others():
        z_up(p, mc).start()
    shares(18, parts)
    for p in others():
        z_up(p, p).wait()
    pair_up = remote(sums.at[core], sums.at[core], core_send, core_recv, "rows", mate)
    pair_up.start()
    pair_up.wait()
    sums_ref[...] = sums[...]

    for p in others():
        self_copy(p, p).wait()
    own.wait()

    def drain(d, _):
        p = lax.rem(me + d, parts)
        share_copy(p, p).wait()
        return 0

    lax.fori_loop(1, parts, drain, 0)


def finish(shares, self_rows, w_own, w_in):
    parts, cap, tile, width = shares.shape
    cols = self_rows.shape[0]
    chips = w_own.shape[0]
    sums = (2, cols) + w_own.shape
    DMA = pltpu.SemaphoreType.DMA
    return pl.pallas_call(
        functools.partial(finish_kernel, parts, cols),
        out_shape=(
            jax.ShapeDtypeStruct(shares.shape, BF16),
            jax.ShapeDtypeStruct(self_rows.shape, BF16),
            jax.ShapeDtypeStruct(sums, BF16),
        ),
        in_specs=[ANY, ANY, VMEM, [VMEM] * len(w_in)],
        out_specs=(ANY, ANY, VMEM),
        scratch_shapes=[
            pltpu.VMEM(w_own.shape, BF16),
            pltpu.VMEM(w_own.shape, BF16),
            pltpu.VMEM(sums, BF16),
            DMA((parts,)), DMA((parts,)), DMA((cols,)), DMA((cols,)), DMA,
            DMA, DMA, DMA((cols,)), DMA((cols,)),
            DMA((chips,)), DMA((chips,)), DMA((chips,)), DMA((chips,)),
        ],
        compiler_params=pltpu.CompilerParams(collective_id=1, has_side_effects=True, vmem_limit_bytes=40 << 20),
        name="finish",
    )(shares, self_rows, w_own, w_in)


def combine_kernel(scale, wanted_ref, self_ref, own_ref, back_ref, sums_ref, out_ref, gs_ref, gn_ref):
    slots = back_ref.shape[0]
    out_ref[...] = self_ref[...].astype(F32) + own_ref[...].astype(F32)

    def add(s, _):
        t = wanted_ref[s]

        @pl.when(t >= 0)
        def _():
            out_ref[t] += back_ref[s].astype(F32)

        return 0

    lax.fori_loop(0, slots, add, 0)
    halves, cols, chips, rows_p, cols_p = sums_ref.shape
    hid = gs_ref.shape[0]
    wide = hid // cols_p
    for half, ref in enumerate((gs_ref, gn_ref)):
        for c in range(cols):
            for q in range(chips):
                at = c * (hid // cols) + (q // wide) * rows_p
                ref[at:at + rows_p, (q % wide) * cols_p:(q % wide + 1) * cols_p] = sums_ref[half, c, q].astype(F32) * scale


def combine(wanted, self_part, own, back, sums, scale):
    hid = own.shape[-1] * sums.shape[1]
    weights = jax.ShapeDtypeStruct((hid, hid), F32)
    return pl.pallas_call(
        functools.partial(combine_kernel, scale),
        out_shape=(jax.ShapeDtypeStruct(own.shape, F32), weights, weights),
        in_specs=[SMEM, VMEM, VMEM, VMEM, VMEM],
        out_specs=(VMEM, VMEM, VMEM),
        compiler_params=pltpu.CompilerParams(vmem_limit_bytes=40 << 20),
        name="combine",
    )(wanted, self_part, own, back, sums)


def body(feats, adj_vals, colref, fetch_ids, w_self, w_neigh, grad_out):
    node_rows, width = feats.shape
    blocks, per_block, tile, _ = adj_vals.shape
    parts = lax.axis_size("rows")
    cols = lax.axis_size("cols")
    cap = fetch_ids.shape[2]
    slots = parts * cap
    hid = width * cols
    scale = 1.0 / math.sqrt(node_rows * parts)
    fetch = jnp.pad(fetch_ids.reshape(parts, cap).T, ((0, 0), (0, 128 - parts)))
    refs = colref.T
    gout = grad_out.reshape(blocks // cols, tile, hid)
    act, self_rows, gagg, w_own, w_send, wanted = layer(
        fetch, refs, feats.reshape(blocks, tile, width), adj_vals, w_self, w_neigh, gout, parts, cols, cap
    )
    w_in = [
        lax.ppermute(w, "cols", [(c, (c + d) % cols) for c in range(cols)]) for d, w in enumerate(w_send, 1)
    ]
    own, shares, act = spread(refs, adj_vals, gagg.reshape(blocks, tile, width), act, slots)
    returned, self_part, sums = finish(shares.reshape(parts, cap, tile, width), self_rows, w_own, w_in)
    grad_feats, grad_self, grad_neigh = combine(
        wanted, self_part.reshape(blocks, tile, width), own,
        returned.reshape(slots, tile, width), sums, scale,
    )
    return act.reshape(grad_out.shape), grad_self, grad_neigh, grad_feats.reshape(node_rows, width)


def solution(mesh):
    in_specs = (
        P("rows", "cols"),
        P("rows", None, None, None),
        P("rows", None),
        P("rows", None, None),
        P(),
        P(),
        P(("rows", "cols"), None),
    )
    out_specs = (P(("rows", "cols"), None), P(), P(), P("rows", "cols"))
    return jax.shard_map(body, mesh=mesh, in_specs=in_specs, out_specs=out_specs, check_vma=False)
```

```python
import functools
import math

import jax
import jax.numpy as jnp
from jax import lax
from jax.experimental import pallas as pl
from jax.experimental.pallas import tpu as pltpu
from jax.sharding import PartitionSpec as P

MESH = pl.DeviceIdType.MESH
ANY = pl.BlockSpec(memory_space=pl.ANY)
VMEM = pl.BlockSpec(memory_space=pltpu.VMEM)
SMEM = pl.BlockSpec(memory_space=pltpu.SMEM)
BF16 = jnp.bfloat16
F32 = jnp.float32


def remote(src, dst, send, recv, axis, peer):
    return pltpu.make_async_remote_copy(
        src_ref=src, dst_ref=dst, send_sem=send, recv_sem=recv,
        device_id={axis: peer}, device_id_type=MESH,
    )


def send_order(parts):
    side = math.isqrt(parts // 2)
    hops = lambda n: min(n, side - n)
    offsets = [(y, x, c) for y in range(side) for x in range(side) for c in range(2)][1:]
    return sorted(offsets, key=lambda o: (-hops(o[0]) - hops(o[1]), o[2]))


def at_offset(me, parts, offset):
    side = math.isqrt(parts // 2)
    dy, dx, dc = offset
    core, chip = lax.rem(me, 2), me // 2
    y, x = lax.rem(chip // side + dy, side), lax.rem(lax.rem(chip, side) + dx, side)
    return (y * side + x) * 2 + (1 - core if dc else core)


def layer_kernel(parts, cols, cap, blocks, per_block, step, fetch_ref, colref_ref, slots_ref, feats_hbm, adj_hbm,
                 w_self_hbm, w_neigh_hbm, gout_hbm, act_ref, selfp_hbm, ret_hbm, own_ref, sums_ref, wanted_ref,
                 pool, own_v, adj_v, stage, agg_v, frows, arows, w_v, gout_v, gagg_v, gagg_in, self_v, gw, from_core, w_half,
                 w_out, w_in, to_chip, from_chip, sums, run_v, sort_v, sort_s, idx_v, idx_s,
                 pool_sem, adj_sem, own_sem, ownv_sem, w_sem, gout_sem, smem_sem, sort_sem,
                 idx_send, idx_recv, tile_send, tile_recv, f_send, f_recv, a_send, a_recv, g_send, g_recv,
                 core_send, core_recv, wz_send, wz_recv, s_send, s_recv, p_send, p_recv,
                 z_send, z_recv, chip_send, chip_recv, up_send, up_recv, pair_send, pair_recv):
    me = lax.axis_index("rows")
    mc = lax.axis_index("cols")
    share = blocks // cols
    groups = share // step
    tile, width = own_v.shape[1:]
    hid = cols * width

    local = [
        pltpu.make_async_copy(feats_hbm, own_v, ownv_sem),
        pltpu.make_async_copy(feats_hbm, pool.at[pl.ds(0, blocks)], pool_sem),
        pltpu.make_async_copy(feats_hbm.at[pl.ds(mc * share, share)], frows.at[mc], own_sem),
        pltpu.make_async_copy(w_self_hbm, w_v.at[pl.ds(0, hid)], w_sem.at[0]),
        pltpu.make_async_copy(w_neigh_hbm, w_v.at[pl.ds(hid, hid)], w_sem.at[1]),
        pltpu.make_async_copy(gout_hbm, gout_v, gout_sem),
    ]
    for q in range(cols):
        part = pl.ds(q * share * per_block, share * per_block)
        local.append(pltpu.make_async_copy(adj_hbm.at[part], adj_v.at[part], adj_sem.at[q]))
    local[0].start()

    barrier = pltpu.get_barrier_semaphore()

    def hello(d, _):
        pl.semaphore_signal(barrier, inc=1, device_id={"rows": lax.rem(me + d, parts)}, device_id_type=MESH)
        return 0

    lax.fori_loop(1, parts, hello, 0)
    for d in range(1, cols):
        pl.semaphore_signal(barrier, inc=1, device_id={"cols": lax.rem(mc + d, cols)}, device_id_type=MESH)
    pl.semaphore_wait(barrier, parts - 1 + cols - 1)

    def ask(d, _):
        p = lax.rem(me + d, parts)
        remote(fetch_ref, idx_v.at[me], idx_send.at[p], idx_recv.at[me], "rows", p).start()
        return 0

    lax.fori_loop(1, parts, ask, 0)
    idx_v[me] = jnp.full(idx_v.shape[1:], -1, jnp.int32)
    local[0].wait()

    def asked(d, _):
        p = lax.rem(me + parts - d, parts)
        remote(fetch_ref, idx_v.at[p], idx_send.at[p], idx_recv.at[p], "rows", p).wait_recv()
        return 0

    lax.fori_loop(1, parts, asked, 0)
    to_smem = pltpu.make_async_copy(idx_v, idx_s, smem_sem)
    to_smem.start()
    to_smem.wait()
    for offset in send_order(parts):
        p = at_offset(me, parts, offset)
        for s in range(cap):
            stage[p, s] = own_v[jnp.maximum(idx_s[p, s, me], 0)]
        remote(stage.at[p], pool.at[pl.ds(blocks + me * cap, cap)], tile_send.at[p], tile_recv.at[me], "rows", p).start()

    for d in range(1, cols):
        p = lax.rem(mc + d, cols)
        remote(own_v.at[pl.ds(p * share, share)], frows.at[mc], f_send.at[p], f_recv.at[mc], "cols", p).start()
    for copy in local[1:]:
        copy.start()

    def want(p, _):
        for s in range(cap):
            wanted_ref[p * cap + s] = idx_s[p, s, me]
        return 0

    lax.fori_loop(0, parts, want, 0)

    refs = blocks * per_block
    key_row = slots_ref[...] * refs + lax.broadcasted_iota(jnp.int32, (1, refs), 1)
    down = lax.broadcasted_iota(jnp.int32, (refs, refs), 0)
    across = lax.broadcasted_iota(jnp.int32, (refs, refs), 1)
    key_col = jnp.sum(jnp.where(down == across, key_row, 0), axis=1, keepdims=True)
    rank_col = jnp.sum(jnp.where(key_row < key_col, 1, 0), axis=1, keepdims=True)
    sort_v[0:1, :] = jnp.sum(jnp.where(rank_col == across, down, 0), axis=0, keepdims=True)
    before = jnp.where(key_col < (across + 1) * refs, 1, 0)
    sort_v[1:2, :] = jnp.sum(before, axis=0, keepdims=True) - 1
    sort_v[2:3, :] = jnp.sum(jnp.where(key_col < across * refs, 0, before), axis=0, keepdims=True)
    to_sort = pltpu.make_async_copy(sort_v, sort_s, sort_sem)
    to_sort.start()
    to_sort.wait()

    pool[pl.ds(blocks + me * cap, cap)] = jnp.zeros((cap,) + pool.shape[1:], BF16)
    for copy in local[1:]:
        copy.wait()
    for d in range(1, cols):
        p = lax.rem(mc + d, cols)
        remote(own_v.at[pl.ds(p * share, share)], frows.at[p], f_send.at[p], f_recv.at[p], "cols", p).wait()

    def given(d, _):
        p = lax.rem(me + parts - d, parts)
        remote(stage.at[p], pool.at[pl.ds(blocks + p * cap, cap)], tile_send.at[p], tile_recv.at[p], "rows", p).wait_recv()
        return 0

    lax.fori_loop(1, parts, given, 0)

    def aggregate(b):
        left = jnp.concatenate([adj_v[b * per_block + k] for k in range(per_block)], axis=1)
        right = jnp.concatenate([pool[colref_ref[k, b]] for k in range(per_block)], axis=0)
        return jnp.dot(left, right, preferred_element_type=F32).astype(BF16)

    def agg_copy(p, slot, i):
        return remote(agg_v.at[p, i], arows.at[slot, i], a_send.at[p, i], a_recv.at[slot, i], "cols", p)

    def back_copy(p, slot, g):
        part = pl.ds(g * step, step)
        return remote(gagg_v.at[p, part], gagg_in.at[slot, part], g_send.at[p, g], g_recv.at[slot, g], "cols", p)

    def tile_round(i):
        def one(d, _):
            p = lax.rem(mc + d, cols)
            agg_v[p, i] = aggregate(p * share + i)
            agg_copy(p, mc, i).start()
            return 0

        lax.fori_loop(1, cols, one, 0)
        arows[mc, i] = aggregate(mc * share + i)

    def dense(g):
        part = pl.ds(g * step, step)
        for j in range(step):
            for d in range(1, cols):
                p = lax.rem(mc + d, cols)
                agg_copy(p, p, g * step + j).wait_recv()

        def rows_of(ref):
            return jnp.concatenate([ref[c, part].reshape(step * tile, width) for c in range(cols)], axis=1)

        both = jnp.concatenate([rows_of(frows), rows_of(arows)], axis=1)
        v = jnp.dot(both, w_v[...], preferred_element_type=F32)
        c0 = math.sqrt(2.0 / math.pi)
        v2 = v * v
        t = jnp.tanh(c0 * v * (1.0 + 0.044715 * v2))
        half = 0.5 * (1.0 + t)
        act_ref[part] = (v * half).astype(BF16).reshape(step, tile, hid)
        slope = half + (0.5 * v) * (1.0 - t * t) * (c0 * (1.0 + 3.0 * 0.044715 * v2))
        grad_pre = (gout_v[part].reshape(step * tile, hid).astype(F32) * slope).astype(BF16)
        nt = (((1,), (1,)), ((), ()))
        out = lax.dot_general(grad_pre, w_v[pl.ds(hid, hid)], nt, preferred_element_type=F32).astype(BF16)
        for c in range(cols):
            gagg_v[c, part] = out[:, c * width:(c + 1) * width].reshape(step, tile, width)
        for d in range(1, cols):
            back_copy(lax.rem(mc + d, cols), mc, g).start()
        gagg_in[mc, part] = gagg_v[mc, part]
        out = lax.dot_general(grad_pre, w_v[pl.ds(0, hid)], nt, preferred_element_type=F32).astype(BF16)
        for c in range(cols):
            self_v[c, part] = out[:, c * width:(c + 1) * width].reshape(step, tile, width)
        sums = lax.dot_general(both, grad_pre, (((0,), (0,)), ((), ())), preferred_element_type=F32)
        gw[...] += sums.reshape(gw.shape)

    def spread(g):
        for d in range(1, cols):
            p = lax.rem(mc + d, cols)
            back_copy(p, p, g).wait_recv()

        def one(n, _):
            c, i = n // step, g * step + lax.rem(n, step)
            at = (c * share + i) * per_block
            grad_t = gagg_in[c, i].T
            for k in range(0, per_block, 2):
                pair = jnp.concatenate([adj_v[at + k], adj_v[at + k + 1]], axis=1)
                out = jnp.dot(grad_t, pair, preferred_element_type=F32).astype(BF16)
                adj_v[at + k] = out[:, :tile]
                adj_v[at + k + 1] = out[:, tile:]
            return 0

        lax.fori_loop(0, cols * step, one, 0)

    gw[...] = jnp.zeros_like(gw)

    def work(g, _):
        @pl.when(g < groups)
        def _():
            for j in range(step):
                tile_round(g * step + j)

        @pl.when((g > 0) & (g <= groups))
        def _():
            dense(g - 1)

        @pl.when(g > 1)
        def _():
            spread(g - 2)

        return 0

    lax.fori_loop(0, groups + 1, work, 0)

    core = lax.rem(me, 2)
    mate = me + 1 - 2 * core
    pair = remote(gw.at[1 - core], from_core, core_send, core_recv, "rows", mate)
    pair.start()
    work(groups + 1, 0)

    def share_copy(p, slot):
        return remote(stage.at[p], ret_hbm.at[slot], s_send.at[p], s_recv.at[slot], "rows", p)

    def self_copy(p, slot):
        return remote(self_v.at[p], selfp_hbm.at[slot], p_send.at[p], p_recv.at[slot], "cols", p)

    def others():
        return [lax.rem(mc + d, cols) for d in range(1, cols)]

    chips = parts // 2
    chip = me // 2

    def over_chips(f):
        def one(d, _):
            f(lax.rem(chip + d, chips))
            return 0

        lax.fori_loop(1, chips, one, 0)

    pair.wait()
    _, _, rows_p, cols_p = w_half.shape
    wide = hid // cols_p
    for c in range(cols):
        for q in range(chips):
            rows = pl.ds(c * (hid // cols) + (q // wide) * rows_p, rows_p)
            lanes = pl.ds((q % wide) * cols_p, cols_p)
            w_half[c, q] = gw[core, rows, lanes] + from_core[rows, lanes]
        w_out[c] = w_half[c].astype(BF16)

    def wz_copy(p, slot):
        return remote(w_out.at[p], w_in.at[slot], wz_send.at[p], wz_recv.at[slot], "cols", p)

    for p in others():
        wz_copy(p, mc).start()
    for p in others():
        self_copy(p, mc).start()
    own_self = pltpu.make_async_copy(self_v.at[mc], selfp_hbm.at[mc], own_sem)
    own_self.start()

    def run(n, carry):
        last_slot, total = carry
        ref = sort_s[0, n]
        slot = colref_ref[lax.rem(ref, per_block), ref // per_block]
        total = jnp.where(slot == last_slot, total, 0.0) + adj_v[ref].astype(F32)
        run_v[n] = total.astype(BF16)
        return slot, total

    lax.fori_loop(0, refs, run, (jnp.int32(-1), jnp.zeros((width, tile), F32)), unroll=4)

    def drain_tiles(d, _):
        p = lax.rem(me + d, parts)
        remote(stage.at[p], pool.at[pl.ds(blocks + p * cap, cap)], tile_send.at[p], tile_recv.at[p], "rows", p).wait_send()
        return 0

    lax.fori_loop(1, parts, drain_tiles, 0)

    def share_of(slot):
        tile_sum = run_v[jnp.maximum(sort_s[1, slot], 0)]
        return jnp.where(sort_s[2, slot] > 0, tile_sum, jnp.zeros_like(tile_sum))

    order = send_order(parts)

    def shares(lo, hi):
        for offset in order[lo:hi]:
            p = at_offset(me, parts, offset)
            for n in range(cap):
                stage[p, n] = share_of(blocks + p * cap + n)
            share_copy(p, me).start()

    for p in others():
        wz_copy(p, p).wait()
    total = w_half[mc]
    for p in others():
        total = total + w_in[p].astype(F32)
    to_chip[...] = total.astype(BF16)

    def chip_copy(q, slot):
        return remote(to_chip.at[q], from_chip.at[slot], chip_send.at[q], chip_recv.at[slot], "rows", 2 * q + core)

    over_chips(lambda q: chip_copy(q, chip).start())
    shares(0, 8)
    from_chip[chip] = to_chip[chip]
    over_chips(lambda q: chip_copy(q, q).wait())
    total = from_chip[0].astype(F32)
    for q in range(1, chips):
        total = total + from_chip[q].astype(F32)
    sums[core, mc, chip] = total.astype(BF16)

    def up_copy(q, slot):
        return remote(sums.at[core, mc, chip], sums.at[core, mc, slot], up_send.at[q], up_recv.at[slot], "rows", 2 * q + core)

    over_chips(lambda q: up_copy(q, chip).start())
    shares(8, 18)
    over_chips(lambda q: up_copy(q, q).wait())

    def z_up(p, slot):
        return remote(sums.at[core, mc], sums.at[core, slot], z_send.at[p], z_recv.at[slot], "cols", p)

    for p in others():
        z_up(p, mc).start()
    shares(18, parts - 1)

    def own_share(t, _):
        own_ref[t] = share_of(t)
        return 0

    lax.fori_loop(0, blocks, own_share, 0)
    for p in others():
        z_up(p, p).wait()
    pair_up = remote(sums.at[core], sums.at[core], pair_send, pair_recv, "rows", mate)
    pair_up.start()
    pair_up.wait()
    sums_ref[...] = sums[...]

    for p in others():
        self_copy(p, p).wait()
    own_self.wait()

    def drain(d, _):
        p = lax.rem(me + d, parts)
        remote(fetch_ref, idx_v.at[p], idx_send.at[p], idx_recv.at[p], "rows", p).wait_send()
        share_copy(p, p).wait()
        return 0

    lax.fori_loop(1, parts, drain, 0)

    def drain_agg(i, _):
        for d in range(1, cols):
            p = lax.rem(mc + d, cols)
            agg_copy(p, p, i).wait_send()
        return 0

    lax.fori_loop(0, share, drain_agg, 0)

    def drain_back(g, _):
        for d in range(1, cols):
            p = lax.rem(mc + d, cols)
            back_copy(p, p, g).wait_send()
        return 0

    lax.fori_loop(0, groups, drain_back, 0)


def layer(fetch, colref, slots, feats, adj, w_self, w_neigh, gout, parts, cols, cap):
    refs, tile, _ = adj.shape
    blocks = feats.shape[0]
    per_block = refs // blocks
    width = feats.shape[-1]
    share = blocks // cols
    hid = cols * width
    step = 2
    groups = share // step
    chips = parts // 2
    piece = (16, 2 * hid * hid // (2 * cols * chips * 16))
    DMA = pltpu.SemaphoreType.DMA
    rows_shape = (cols, share, tile, width)
    return pl.pallas_call(
        functools.partial(layer_kernel, parts, cols, cap, blocks, per_block, step),
        out_shape=(
            jax.ShapeDtypeStruct(gout.shape, BF16),
            jax.ShapeDtypeStruct(rows_shape, BF16),
            jax.ShapeDtypeStruct((parts, cap, width, tile), BF16),
            jax.ShapeDtypeStruct((blocks, width, tile), BF16),
            jax.ShapeDtypeStruct((2, cols, chips) + piece, BF16),
            jax.ShapeDtypeStruct((parts * cap,), jnp.int32),
        ),
        in_specs=[VMEM, SMEM, VMEM, ANY, ANY, ANY, ANY, ANY],
        out_specs=(VMEM, ANY, ANY, VMEM, VMEM, SMEM),
        scratch_shapes=[
            pltpu.VMEM((blocks + parts * cap, tile, width), BF16),
            pltpu.VMEM(feats.shape, BF16),
            pltpu.VMEM(adj.shape, BF16),
            pltpu.VMEM((parts, cap, tile, width), BF16),
            pltpu.VMEM(rows_shape, BF16),
            pltpu.VMEM(rows_shape, BF16),
            pltpu.VMEM(rows_shape, BF16),
            pltpu.VMEM((2 * hid, hid), BF16),
            pltpu.VMEM(gout.shape, BF16),
            pltpu.VMEM(rows_shape, BF16),
            pltpu.VMEM(rows_shape, BF16),
            pltpu.VMEM(rows_shape, BF16),
            pltpu.VMEM((2, hid, hid), F32),
            pltpu.VMEM((hid, hid), F32),
            pltpu.VMEM((cols, chips) + piece, F32),
            pltpu.VMEM((cols, chips) + piece, BF16),
            pltpu.VMEM((cols, chips) + piece, BF16),
            pltpu.VMEM((chips,) + piece, BF16),
            pltpu.VMEM((chips,) + piece, BF16),
            pltpu.VMEM((2, cols, chips) + piece, BF16),
            pltpu.VMEM((refs, width, tile), BF16),
            pltpu.VMEM((8, refs), jnp.int32),
            pltpu.SMEM((8, refs), jnp.int32),
            pltpu.VMEM((parts,) + fetch.shape, jnp.int32),
            pltpu.SMEM((parts,) + fetch.shape, jnp.int32),
            DMA, DMA((cols,)), DMA, DMA, DMA((2,)), DMA, DMA, DMA,
            DMA((parts,)), DMA((parts,)), DMA((parts,)), DMA((parts,)),
            DMA((cols,)), DMA((cols,)), DMA((cols, share)), DMA((cols, share)),
            DMA((cols, groups)), DMA((cols, groups)), DMA, DMA,
            DMA((cols,)), DMA((cols,)), DMA((parts,)), DMA((parts,)), DMA((cols,)), DMA((cols,)),
            DMA((cols,)), DMA((cols,)), DMA((chips,)), DMA((chips,)), DMA((chips,)), DMA((chips,)), DMA, DMA,
        ],
        compiler_params=pltpu.CompilerParams(collective_id=0, has_side_effects=True, vmem_limit_bytes=63 << 20),
        name="layer",
    )(fetch, colref, slots, feats, adj, w_self, w_neigh, gout)


def combine_kernel(scale, wanted_ref, self_ref, own_ref, back_ref, sums_ref, act_ref,
                   out_ref, gs_ref, gn_ref, act_out_ref, total):
    slots = back_ref.shape[0]
    act_out_ref[...] = act_ref[...]
    total[...] = own_ref[...].astype(F32)

    def add(s, _):
        t = wanted_ref[s]

        @pl.when(t >= 0)
        def _():
            total[t] += back_ref[s].astype(F32)

        return 0

    lax.fori_loop(0, slots, add, 0)

    def put(t, _):
        out_ref[t] = self_ref[t].astype(F32) + total[t].T
        return 0

    lax.fori_loop(0, total.shape[0], put, 0, unroll=4)
    halves, cols, chips, rows_p, cols_p = sums_ref.shape
    hid = gs_ref.shape[0]
    wide = hid // cols_p
    for half, ref in enumerate((gs_ref, gn_ref)):
        for c in range(cols):
            for q in range(chips):
                at = c * (hid // cols) + (q // wide) * rows_p
                ref[at:at + rows_p, (q % wide) * cols_p:(q % wide + 1) * cols_p] = sums_ref[half, c, q].astype(F32) * scale


def combine(wanted, self_part, own, back, sums, act, scale):
    hid = self_part.shape[-1] * sums.shape[1]
    weights = jax.ShapeDtypeStruct((hid, hid), F32)
    return pl.pallas_call(
        functools.partial(combine_kernel, scale),
        out_shape=(jax.ShapeDtypeStruct(self_part.shape, F32), weights, weights, jax.ShapeDtypeStruct(act.shape, BF16)),
        in_specs=[SMEM, VMEM, VMEM, VMEM, VMEM, VMEM],
        out_specs=(VMEM, VMEM, VMEM, VMEM),
        scratch_shapes=[pltpu.VMEM(own.shape, F32)],
        compiler_params=pltpu.CompilerParams(vmem_limit_bytes=40 << 20),
        name="combine",
    )(wanted, self_part, own, back, sums, act)


def body(feats, adj_vals, colref, fetch_ids, w_self, w_neigh, grad_out):
    node_rows, width = feats.shape
    blocks, per_block, tile, _ = adj_vals.shape
    parts = lax.axis_size("rows")
    cols = lax.axis_size("cols")
    cap = fetch_ids.shape[2]
    refs = blocks * per_block
    hid = width * cols
    scale = 1.0 / math.sqrt(node_rows * parts)
    fetch = jnp.pad(fetch_ids.reshape(parts, cap).T, ((0, 0), (0, 128 - parts)))
    gout = grad_out.reshape(blocks // cols, tile, hid)
    act, self_part, returned, own, sums, wanted = layer(
        fetch, colref.T, colref.reshape(1, refs), feats.reshape(blocks, tile, width),
        adj_vals.reshape(refs, tile, tile), w_self, w_neigh, gout, parts, cols, cap,
    )
    grad_feats, grad_self, grad_neigh, act = combine(
        wanted, self_part.reshape(blocks, tile, width), own, returned.reshape(parts * cap, width, tile), sums, act, scale
    )
    return act.reshape(grad_out.shape), grad_self, grad_neigh, grad_feats.reshape(node_rows, width)


def solution(mesh):
    in_specs = (
        P("rows", "cols"),
        P("rows", None, None, None),
        P("rows", None),
        P("rows", None, None),
        P(),
        P(),
        P(("rows", "cols"), None),
    )
    out_specs = (P(("rows", "cols"), None), P(), P(), P("rows", "cols"))
    return jax.shard_map(body, mesh=mesh, in_specs=in_specs, out_specs=out_specs, check_vma=False)
```

```python
import functools
import math

import jax
import jax.numpy as jnp
from jax import lax
from jax.experimental import pallas as pl
from jax.experimental.pallas import tpu as pltpu
from jax.sharding import PartitionSpec as P

MESH = pl.DeviceIdType.MESH
ANY = pl.BlockSpec(memory_space=pl.ANY)
VMEM = pl.BlockSpec(memory_space=pltpu.VMEM)
SMEM = pl.BlockSpec(memory_space=pltpu.SMEM)
BF16 = jnp.bfloat16
F32 = jnp.float32


def remote(src, dst, send, recv, axis, peer):
    return pltpu.make_async_remote_copy(
        src_ref=src, dst_ref=dst, send_sem=send, recv_sem=recv,
        device_id={axis: peer}, device_id_type=MESH,
    )


def send_order(parts):
    side = math.isqrt(parts // 2)
    hops = lambda n: min(n, side - n)
    offsets = [(y, x, c) for y in range(side) for x in range(side) for c in range(2)][1:]
    return sorted(offsets, key=lambda o: (-hops(o[0]) - hops(o[1]), o[2]))


def at_offset(me, parts, offset):
    side = math.isqrt(parts // 2)
    dy, dx, dc = offset
    core, chip = lax.rem(me, 2), me // 2
    y, x = lax.rem(chip // side + dy, side), lax.rem(lax.rem(chip, side) + dx, side)
    return (y * side + x) * 2 + (1 - core if dc else core)


def layer_kernel(parts, cols, cap, blocks, per_block, step, fetch_ref, colref_ref, slots_ref, feats_hbm, adj_hbm,
                 w_self_hbm, w_neigh_hbm, gout_hbm, act_hbm, selfp_hbm, ret_hbm, own_hbm, sums_ref, wanted_ref,
                 act_v, pool, own_v, adj_v, stage, agg_v, frows, arows, w_v, gout_v, gagg_v, gagg_in, self_v, gw, from_core, w_half,
                 w_out, w_in, to_chip, from_chip, sums, run_v, sort_v, sort_s, idx_v, idx_s,
                 pool_sem, adj_sem, own_sem, ownv_sem, w_sem, gout_sem, smem_sem, sort_sem,
                 idx_send, idx_recv, tile_send, tile_recv, f_send, f_recv, a_send, a_recv, g_send, g_recv,
                 core_send, core_recv, wz_send, wz_recv, s_send, s_recv, p_send, p_recv,
                 z_send, z_recv, chip_send, chip_recv, up_send, up_recv, pair_send, pair_recv):
    me = lax.axis_index("rows")
    mc = lax.axis_index("cols")
    share = blocks // cols
    groups = share // step
    tile, width = own_v.shape[1:]
    hid = cols * width

    local = [
        pltpu.make_async_copy(feats_hbm, own_v, ownv_sem),
        pltpu.make_async_copy(feats_hbm, pool.at[pl.ds(0, blocks)], pool_sem),
        pltpu.make_async_copy(feats_hbm.at[pl.ds(mc * share, share)], frows.at[mc], own_sem),
        pltpu.make_async_copy(w_self_hbm, w_v.at[pl.ds(0, hid)], w_sem.at[0]),
        pltpu.make_async_copy(w_neigh_hbm, w_v.at[pl.ds(hid, hid)], w_sem.at[1]),
        pltpu.make_async_copy(gout_hbm, gout_v, gout_sem),
    ]
    for q in range(cols):
        part = pl.ds(q * share * per_block, share * per_block)
        local.append(pltpu.make_async_copy(adj_hbm.at[part], adj_v.at[part], adj_sem.at[q]))
    local[0].start()

    barrier = pltpu.get_barrier_semaphore()

    def hello(d, _):
        pl.semaphore_signal(barrier, inc=1, device_id={"rows": lax.rem(me + d, parts)}, device_id_type=MESH)
        return 0

    lax.fori_loop(1, parts, hello, 0)
    for d in range(1, cols):
        pl.semaphore_signal(barrier, inc=1, device_id={"cols": lax.rem(mc + d, cols)}, device_id_type=MESH)
    pl.semaphore_wait(barrier, parts - 1 + cols - 1)

    def ask(d, _):
        p = lax.rem(me + d, parts)
        remote(fetch_ref, idx_v.at[me], idx_send.at[p], idx_recv.at[me], "rows", p).start()
        return 0

    lax.fori_loop(1, parts, ask, 0)
    idx_v[me] = jnp.full(idx_v.shape[1:], -1, jnp.int32)
    local[0].wait()

    def asked(d, _):
        p = lax.rem(me + parts - d, parts)
        remote(fetch_ref, idx_v.at[p], idx_send.at[p], idx_recv.at[p], "rows", p).wait_recv()
        return 0

    lax.fori_loop(1, parts, asked, 0)
    to_smem = pltpu.make_async_copy(idx_v, idx_s, smem_sem)
    to_smem.start()
    to_smem.wait()
    for offset in send_order(parts):
        p = at_offset(me, parts, offset)
        for s in range(cap):
            stage[p, s] = own_v[jnp.maximum(idx_s[p, s, me], 0)]
        remote(stage.at[p], pool.at[pl.ds(blocks + me * cap, cap)], tile_send.at[p], tile_recv.at[me], "rows", p).start()

    for d in range(1, cols):
        p = lax.rem(mc + d, cols)
        remote(own_v.at[pl.ds(p * share, share)], frows.at[mc], f_send.at[p], f_recv.at[mc], "cols", p).start()
    for copy in local[1:]:
        copy.start()

    def want(p, _):
        for s in range(cap):
            wanted_ref[p * cap + s] = idx_s[p, s, me]
        return 0

    lax.fori_loop(0, parts, want, 0)

    refs = blocks * per_block
    grid = (per_block, refs)
    place = lax.broadcasted_iota(jnp.int32, grid, 1)
    slots = jnp.zeros(grid, jnp.int32)
    table = slots_ref[...]
    for b in range(blocks):
        slots = jnp.where(place // per_block == b, table[:, b:b + 1], slots)
    slots = jnp.where(lax.rem(place, per_block) == lax.broadcasted_iota(jnp.int32, grid, 0), slots, 0)
    key_row = jnp.sum(slots, axis=0, keepdims=True) * refs + lax.broadcasted_iota(jnp.int32, (1, refs), 1)
    down = lax.broadcasted_iota(jnp.int32, (refs, refs), 0)
    across = lax.broadcasted_iota(jnp.int32, (refs, refs), 1)
    key_col = jnp.sum(jnp.where(down == across, key_row, 0), axis=1, keepdims=True)
    rank_col = jnp.sum(jnp.where(key_row < key_col, 1, 0), axis=1, keepdims=True)
    sort_v[0:1, :] = jnp.sum(jnp.where(rank_col == across, down, 0), axis=0, keepdims=True)
    before = jnp.where(key_col < (across + 1) * refs, 1, 0)
    sort_v[1:2, :] = jnp.sum(before, axis=0, keepdims=True) - 1
    sort_v[2:3, :] = jnp.sum(jnp.where(key_col < across * refs, 0, before), axis=0, keepdims=True)
    to_sort = pltpu.make_async_copy(sort_v, sort_s, sort_sem)
    to_sort.start()
    to_sort.wait()

    pool[pl.ds(blocks + me * cap, cap)] = jnp.zeros((cap,) + pool.shape[1:], BF16)
    for copy in local[1:]:
        copy.wait()
    for d in range(1, cols):
        p = lax.rem(mc + d, cols)
        remote(own_v.at[pl.ds(p * share, share)], frows.at[p], f_send.at[p], f_recv.at[p], "cols", p).wait()

    def given(d, _):
        p = lax.rem(me + parts - d, parts)
        remote(stage.at[p], pool.at[pl.ds(blocks + p * cap, cap)], tile_send.at[p], tile_recv.at[p], "rows", p).wait_recv()
        return 0

    lax.fori_loop(1, parts, given, 0)

    def aggregate(b):
        left = jnp.concatenate([adj_v[b * per_block + k] for k in range(per_block)], axis=1)
        right = jnp.concatenate([pool[colref_ref[k, b]] for k in range(per_block)], axis=0)
        return jnp.dot(left, right, preferred_element_type=F32).astype(BF16)

    def agg_copy(p, slot, i):
        return remote(agg_v.at[p, i], arows.at[slot, i], a_send.at[p, i], a_recv.at[slot, i], "cols", p)

    def back_copy(p, slot, g):
        part = pl.ds(g * step, step)
        return remote(gagg_v.at[p, part], gagg_in.at[slot, part], g_send.at[p, g], g_recv.at[slot, g], "cols", p)

    def tile_round(i):
        def one(d, _):
            p = lax.rem(mc + d, cols)
            agg_v[p, i] = aggregate(p * share + i)
            agg_copy(p, mc, i).start()
            return 0

        lax.fori_loop(1, cols, one, 0)
        arows[mc, i] = aggregate(mc * share + i)

    def dense(g):
        part = pl.ds(g * step, step)
        for j in range(step):
            for d in range(1, cols):
                p = lax.rem(mc + d, cols)
                agg_copy(p, p, g * step + j).wait_recv()

        def rows_of(ref):
            return jnp.concatenate([ref[c, part].reshape(step * tile, width) for c in range(cols)], axis=1)

        both = jnp.concatenate([rows_of(frows), rows_of(arows)], axis=1)
        v = jnp.dot(both, w_v[...], preferred_element_type=F32)
        c0 = math.sqrt(2.0 / math.pi)
        v2 = v * v
        t = jnp.tanh(c0 * v * (1.0 + 0.044715 * v2))
        half = 0.5 * (1.0 + t)
        act_v[part] = (v * half).astype(BF16).reshape(step, tile, hid)
        slope = half + (0.5 * v) * (1.0 - t * t) * (c0 * (1.0 + 3.0 * 0.044715 * v2))
        grad_pre = (gout_v[part].reshape(step * tile, hid).astype(F32) * slope).astype(BF16)
        nt = (((1,), (1,)), ((), ()))
        out = lax.dot_general(grad_pre, w_v[pl.ds(hid, hid)], nt, preferred_element_type=F32).astype(BF16)
        for c in range(cols):
            gagg_v[c, part] = out[:, c * width:(c + 1) * width].reshape(step, tile, width)
        for d in range(1, cols):
            back_copy(lax.rem(mc + d, cols), mc, g).start()
        gagg_in[mc, part] = gagg_v[mc, part]
        out = lax.dot_general(grad_pre, w_v[pl.ds(0, hid)], nt, preferred_element_type=F32).astype(BF16)
        for c in range(cols):
            self_v[c, part] = out[:, c * width:(c + 1) * width].reshape(step, tile, width)
        sums = lax.dot_general(both, grad_pre, (((0,), (0,)), ((), ())), preferred_element_type=F32)
        gw[...] += sums.reshape(gw.shape)

    def spread(g):
        for d in range(1, cols):
            p = lax.rem(mc + d, cols)
            back_copy(p, p, g).wait_recv()

        def one(n, _):
            c, i = n // step, g * step + lax.rem(n, step)
            at = (c * share + i) * per_block
            grad_t = gagg_in[c, i].T
            for k in range(0, per_block, 2):
                pair = jnp.concatenate([adj_v[at + k], adj_v[at + k + 1]], axis=1)
                out = jnp.dot(grad_t, pair, preferred_element_type=F32).astype(BF16)
                adj_v[at + k] = out[:, :tile]
                adj_v[at + k + 1] = out[:, tile:]
            return 0

        lax.fori_loop(0, cols * step, one, 0)

    gw[...] = jnp.zeros_like(gw)

    def work(g, _):
        @pl.when(g < groups)
        def _():
            for j in range(step):
                tile_round(g * step + j)

        @pl.when((g > 0) & (g <= groups))
        def _():
            dense(g - 1)

        @pl.when(g > 1)
        def _():
            spread(g - 2)

        return 0

    lax.fori_loop(0, groups + 1, work, 0)

    core = lax.rem(me, 2)
    mate = me + 1 - 2 * core
    pair = remote(gw.at[1 - core], from_core, core_send, core_recv, "rows", mate)
    pair.start()
    act_out = pltpu.make_async_copy(act_v, act_hbm, gout_sem)
    act_out.start()

    def share_copy(p, slot):
        return remote(stage.at[p], ret_hbm.at[slot], s_send.at[p], s_recv.at[slot], "rows", p)

    def self_copy(p, slot):
        return remote(self_v.at[p], selfp_hbm.at[slot], p_send.at[p], p_recv.at[slot], "cols", p)

    def others():
        return [lax.rem(mc + d, cols) for d in range(1, cols)]

    chips = parts // 2
    chip = me // 2

    def over_chips(f):
        def one(d, _):
            f(lax.rem(chip + d, chips))
            return 0

        lax.fori_loop(1, chips, one, 0)

    pair.wait()
    _, _, rows_p, cols_p = w_half.shape
    wide = hid // cols_p
    for c in range(cols):
        for q in range(chips):
            rows = pl.ds(c * (hid // cols) + (q // wide) * rows_p, rows_p)
            lanes = pl.ds((q % wide) * cols_p, cols_p)
            w_half[c, q] = gw[core, rows, lanes] + from_core[rows, lanes]
        w_out[c] = w_half[c].astype(BF16)

    def wz_copy(p, slot):
        return remote(w_out.at[p], w_in.at[slot], wz_send.at[p], wz_recv.at[slot], "cols", p)

    for p in others():
        wz_copy(p, mc).start()
    for p in others():
        self_copy(p, mc).start()
    own_self = pltpu.make_async_copy(self_v.at[mc], selfp_hbm.at[mc], own_sem)
    own_self.start()
    work(groups + 1, 0)

    def run(n, carry):
        last_slot, total = carry
        ref = sort_s[0, n]
        slot = colref_ref[lax.rem(ref, per_block), ref // per_block]
        total = jnp.where(slot == last_slot, total, 0.0) + adj_v[ref].astype(F32)
        run_v[n] = total.astype(BF16)
        return slot, total

    lax.fori_loop(0, refs, run, (jnp.int32(-1), jnp.zeros((width, tile), F32)), unroll=4)

    def drain_tiles(d, _):
        p = lax.rem(me + d, parts)
        remote(stage.at[p], pool.at[pl.ds(blocks + p * cap, cap)], tile_send.at[p], tile_recv.at[p], "rows", p).wait_send()
        return 0

    lax.fori_loop(1, parts, drain_tiles, 0)

    def share_of(slot):
        tile_sum = run_v[jnp.maximum(sort_s[1, slot], 0)]
        return jnp.where(sort_s[2, slot] > 0, tile_sum, jnp.zeros_like(tile_sum))

    order = send_order(parts)

    def shares(lo, hi):
        for offset in order[lo:hi]:
            p = at_offset(me, parts, offset)
            for n in range(cap):
                stage[p, n] = share_of(blocks + p * cap + n)
            share_copy(p, me).start()

    for p in others():
        wz_copy(p, p).wait()
    total = w_half[mc]
    for p in others():
        total = total + w_in[p].astype(F32)
    to_chip[...] = total.astype(BF16)

    def chip_copy(q, slot):
        return remote(to_chip.at[q], from_chip.at[slot], chip_send.at[q], chip_recv.at[slot], "rows", 2 * q + core)

    over_chips(lambda q: chip_copy(q, chip).start())
    shares(0, 7)
    from_chip[chip] = to_chip[chip]
    over_chips(lambda q: chip_copy(q, q).wait())
    total = from_chip[0].astype(F32)
    for q in range(1, chips):
        total = total + from_chip[q].astype(F32)
    sums[core, mc, chip] = total.astype(BF16)

    def up_copy(q, slot):
        return remote(sums.at[core, mc, chip], sums.at[core, mc, slot], up_send.at[q], up_recv.at[slot], "rows", 2 * q + core)

    over_chips(lambda q: up_copy(q, chip).start())
    shares(7, 14)
    over_chips(lambda q: up_copy(q, q).wait())

    def z_up(p, slot):
        return remote(sums.at[core, mc], sums.at[core, slot], z_send.at[p], z_recv.at[slot], "cols", p)

    for p in others():
        z_up(p, mc).start()
    shares(14, parts - 1)

    def own_share(t, _):
        pool[t] = share_of(t)
        return 0

    lax.fori_loop(0, blocks, own_share, 0)
    own_out = pltpu.make_async_copy(pool.at[pl.ds(0, blocks)], own_hbm, pool_sem)
    own_out.start()
    for p in others():
        z_up(p, p).wait()
    pair_up = remote(sums.at[core], sums.at[core], pair_send, pair_recv, "rows", mate)
    pair_up.start()
    pair_up.wait()
    sums_ref[...] = sums[...]

    for p in others():
        self_copy(p, p).wait()
    own_self.wait()
    own_out.wait()
    act_out.wait()

    def drain(d, _):
        p = lax.rem(me + d, parts)
        remote(fetch_ref, idx_v.at[p], idx_send.at[p], idx_recv.at[p], "rows", p).wait_send()
        share_copy(p, p).wait()
        return 0

    lax.fori_loop(1, parts, drain, 0)

    def drain_agg(i, _):
        for d in range(1, cols):
            p = lax.rem(mc + d, cols)
            agg_copy(p, p, i).wait_send()
        return 0

    lax.fori_loop(0, share, drain_agg, 0)

    def drain_back(g, _):
        for d in range(1, cols):
            p = lax.rem(mc + d, cols)
            back_copy(p, p, g).wait_send()
        return 0

    lax.fori_loop(0, groups, drain_back, 0)


def layer(fetch, colref, slots, feats, adj, w_self, w_neigh, gout, parts, cols, cap):
    refs, tile, _ = adj.shape
    blocks = feats.shape[0]
    per_block = refs // blocks
    width = feats.shape[-1]
    share = blocks // cols
    hid = cols * width
    step = 2
    groups = share // step
    chips = parts // 2
    piece = (16, 2 * hid * hid // (2 * cols * chips * 16))
    DMA = pltpu.SemaphoreType.DMA
    rows_shape = (cols, share, tile, width)
    return pl.pallas_call(
        functools.partial(layer_kernel, parts, cols, cap, blocks, per_block, step),
        out_shape=(
            jax.ShapeDtypeStruct(gout.shape, BF16),
            jax.ShapeDtypeStruct(rows_shape, BF16),
            jax.ShapeDtypeStruct((parts, cap, width, tile), BF16),
            jax.ShapeDtypeStruct((blocks, width, tile), BF16),
            jax.ShapeDtypeStruct((2, cols, chips) + piece, BF16),
            jax.ShapeDtypeStruct((parts * cap,), jnp.int32),
        ),
        in_specs=[VMEM, SMEM, VMEM, ANY, ANY, ANY, ANY, ANY],
        out_specs=(ANY, ANY, ANY, ANY, VMEM, SMEM),
        scratch_shapes=[
            pltpu.VMEM(gout.shape, BF16),
            pltpu.VMEM((blocks + parts * cap, tile, width), BF16),
            pltpu.VMEM(feats.shape, BF16),
            pltpu.VMEM(adj.shape, BF16),
            pltpu.VMEM((parts, cap, tile, width), BF16),
            pltpu.VMEM(rows_shape, BF16),
            pltpu.VMEM(rows_shape, BF16),
            pltpu.VMEM(rows_shape, BF16),
            pltpu.VMEM((2 * hid, hid), BF16),
            pltpu.VMEM(gout.shape, BF16),
            pltpu.VMEM(rows_shape, BF16),
            pltpu.VMEM(rows_shape, BF16),
            pltpu.VMEM(rows_shape, BF16),
            pltpu.VMEM((2, hid, hid), F32),
            pltpu.VMEM((hid, hid), F32),
            pltpu.VMEM((cols, chips) + piece, F32),
            pltpu.VMEM((cols, chips) + piece, BF16),
            pltpu.VMEM((cols, chips) + piece, BF16),
            pltpu.VMEM((chips,) + piece, BF16),
            pltpu.VMEM((chips,) + piece, BF16),
            pltpu.VMEM((2, cols, chips) + piece, BF16),
            pltpu.VMEM((refs, width, tile), BF16),
            pltpu.VMEM((8, refs), jnp.int32),
            pltpu.SMEM((8, refs), jnp.int32),
            pltpu.VMEM((parts,) + fetch.shape, jnp.int32),
            pltpu.SMEM((parts,) + fetch.shape, jnp.int32),
            DMA, DMA((cols,)), DMA, DMA, DMA((2,)), DMA, DMA, DMA,
            DMA((parts,)), DMA((parts,)), DMA((parts,)), DMA((parts,)),
            DMA((cols,)), DMA((cols,)), DMA((cols, share)), DMA((cols, share)),
            DMA((cols, groups)), DMA((cols, groups)), DMA, DMA,
            DMA((cols,)), DMA((cols,)), DMA((parts,)), DMA((parts,)), DMA((cols,)), DMA((cols,)),
            DMA((cols,)), DMA((cols,)), DMA((chips,)), DMA((chips,)), DMA((chips,)), DMA((chips,)), DMA, DMA,
        ],
        compiler_params=pltpu.CompilerParams(collective_id=0, has_side_effects=True, vmem_limit_bytes=63 << 20),
        name="layer",
    )(fetch, colref, slots, feats, adj, w_self, w_neigh, gout)


def combine_kernel(scale, wanted_ref, self_hbm, own_hbm, back_hbm, sums_hbm, act_hbm,
                   out_hbm, gs_hbm, gn_hbm, act_out_hbm,
                   self_v, own_v, back_v, sums_v, out_v, weights, total, in_sem, out_sem):
    moves = [
        pltpu.make_async_copy(src, dst, in_sem.at[n])
        for n, (src, dst) in enumerate(
            ((own_hbm, own_v), (back_hbm, back_v), (sums_hbm, sums_v), (self_hbm, self_v), (act_hbm, act_out_hbm))
        )
    ]
    for move in moves:
        move.start()
    moves[0].wait()
    total[...] = own_v[...].astype(F32)
    moves[1].wait()

    def add(s, _):
        t = wanted_ref[s]

        @pl.when(t >= 0)
        def _():
            total[t] += back_v[s].astype(F32)

        return 0

    lax.fori_loop(0, back_v.shape[0], add, 0)
    moves[2].wait()
    halves, cols, chips, rows_p, cols_p = sums_v.shape
    hid = weights.shape[1]
    wide = hid // cols_p
    for half in range(halves):
        for c in range(cols):
            for q in range(chips):
                at = c * (hid // cols) + (q // wide) * rows_p
                piece = sums_v[half, c, q].astype(F32) * scale
                weights[half, at:at + rows_p, (q % wide) * cols_p:(q % wide + 1) * cols_p] = piece
    done = [
        pltpu.make_async_copy(weights.at[half], ref, out_sem.at[half]) for half, ref in enumerate((gs_hbm, gn_hbm))
    ]
    for move in done:
        move.start()
    moves[3].wait()
    blocks = total.shape[0]
    chunks = 4
    size = blocks // chunks
    for n in range(chunks):
        def put(t, _):
            out_v[t] = self_v[t].astype(F32) + total[t].T
            return 0

        lax.fori_loop(n * size, (n + 1) * size, put, 0, unroll=4)
        part = pl.ds(n * size, size)
        done.append(pltpu.make_async_copy(out_v.at[part], out_hbm.at[part], out_sem.at[halves + n]))
        done[-1].start()
    moves[4].wait()
    for move in done:
        move.wait()


def combine(wanted, self_part, own, back, sums, act, scale):
    hid = self_part.shape[-1] * sums.shape[1]
    weights = jax.ShapeDtypeStruct((hid, hid), F32)
    return pl.pallas_call(
        functools.partial(combine_kernel, scale),
        out_shape=(jax.ShapeDtypeStruct(self_part.shape, F32), weights, weights, jax.ShapeDtypeStruct(act.shape, BF16)),
        in_specs=[SMEM, ANY, ANY, ANY, ANY, ANY],
        out_specs=(ANY, ANY, ANY, ANY),
        scratch_shapes=[
            pltpu.VMEM(self_part.shape, BF16),
            pltpu.VMEM(own.shape, BF16),
            pltpu.VMEM(back.shape, BF16),
            pltpu.VMEM(sums.shape, BF16),
            pltpu.VMEM(self_part.shape, F32),
            pltpu.VMEM((2, hid, hid), F32),
            pltpu.VMEM(own.shape, F32),
            pltpu.SemaphoreType.DMA((5,)),
            pltpu.SemaphoreType.DMA((6,)),
        ],
        compiler_params=pltpu.CompilerParams(vmem_limit_bytes=62 << 20),
        name="combine",
    )(wanted, self_part, own, back, sums, act)


def body(feats, adj_vals, colref, fetch_ids, w_self, w_neigh, grad_out):
    node_rows, width = feats.shape
    blocks, per_block, tile, _ = adj_vals.shape
    parts = lax.axis_size("rows")
    cols = lax.axis_size("cols")
    cap = fetch_ids.shape[2]
    refs = blocks * per_block
    hid = width * cols
    scale = 1.0 / math.sqrt(node_rows * parts)
    fetch = jnp.pad(fetch_ids.reshape(parts, cap).T, ((0, 0), (0, 128 - parts)))
    gout = grad_out.reshape(blocks // cols, tile, hid)
    act, self_part, returned, own, sums, wanted = layer(
        fetch, colref.T, colref.T, feats.reshape(blocks, tile, width),
        adj_vals.reshape(refs, tile, tile), w_self, w_neigh, gout, parts, cols, cap,
    )
    grad_feats, grad_self, grad_neigh, act = combine(
        wanted, self_part.reshape(blocks, tile, width), own, returned.reshape(parts * cap, width, tile), sums, act, scale
    )
    return act.reshape(grad_out.shape), grad_self, grad_neigh, grad_feats.reshape(node_rows, width)


def solution(mesh):
    in_specs = (
        P("rows", "cols"),
        P("rows", None, None, None),
        P("rows", None),
        P("rows", None, None),
        P(),
        P(),
        P(("rows", "cols"), None),
    )
    out_specs = (P(("rows", "cols"), None), P(), P(), P("rows", "cols"))
    return jax.shard_map(body, mesh=mesh, in_specs=in_specs, out_specs=out_specs, check_vma=False)
```

```python
import functools
import math

import jax
import jax.numpy as jnp
from jax import lax
from jax.experimental import pallas as pl
from jax.experimental.pallas import tpu as pltpu
from jax.sharding import PartitionSpec as P

MESH = pl.DeviceIdType.MESH
ANY = pl.BlockSpec(memory_space=pl.ANY)
VMEM = pl.BlockSpec(memory_space=pltpu.VMEM)
SMEM = pl.BlockSpec(memory_space=pltpu.SMEM)
BF16 = jnp.bfloat16
F32 = jnp.float32


def remote(src, dst, send, recv, axis, peer):
    return pltpu.make_async_remote_copy(
        src_ref=src, dst_ref=dst, send_sem=send, recv_sem=recv,
        device_id={axis: peer}, device_id_type=MESH,
    )


def send_order(parts):
    side = math.isqrt(parts // 2)
    hops = lambda n: min(n, side - n)
    offsets = [(y, x, c) for y in range(side) for x in range(side) for c in range(2)][1:]
    return sorted(offsets, key=lambda o: (-hops(o[0]) - hops(o[1]), o[2]))


def at_offset(me, parts, offset):
    side = math.isqrt(parts // 2)
    dy, dx, dc = offset
    core, chip = lax.rem(me, 2), me // 2
    y, x = lax.rem(chip // side + dy, side), lax.rem(lax.rem(chip, side) + dx, side)
    return (y * side + x) * 2 + (1 - core if dc else core)


def layer_kernel(parts, cols, cap, blocks, per_block, step, fetch_ref, colref_ref, slots_ref, feats_hbm, adj_hbm,
                 w_self_hbm, w_neigh_hbm, gout_hbm, act_hbm, selfp_hbm, ret_hbm, own_hbm, sums_ref, wanted_ref,
                 act_v, pool, own_v, adj_v, stage, agg_v, frows, arows, w_v, gout_v, gagg_v, gagg_in, self_v, gw, from_core, w_half,
                 w_out, w_in, to_chip, from_chip, sums, run_v, sort_v, sort_s, idx_v, idx_s,
                 pool_sem, adj_sem, own_sem, ownv_sem, w_sem, gout_sem, smem_sem, sort_sem,
                 idx_send, idx_recv, tile_send, tile_recv, f_send, f_recv, a_send, a_recv, g_send, g_recv,
                 core_send, core_recv, wz_send, wz_recv, s_send, s_recv, p_send, p_recv,
                 z_send, z_recv, chip_send, chip_recv, up_send, up_recv, pair_send, pair_recv):
    me = lax.axis_index("rows")
    mc = lax.axis_index("cols")
    share = blocks // cols
    groups = share // step
    tile, width = own_v.shape[1:]
    hid = cols * width

    local = [
        pltpu.make_async_copy(feats_hbm, own_v, ownv_sem),
        pltpu.make_async_copy(feats_hbm, pool.at[pl.ds(0, blocks)], pool_sem),
        pltpu.make_async_copy(feats_hbm.at[pl.ds(mc * share, share)], frows.at[mc], own_sem),
        pltpu.make_async_copy(w_self_hbm, w_v.at[pl.ds(0, hid)], w_sem.at[0]),
        pltpu.make_async_copy(w_neigh_hbm, w_v.at[pl.ds(hid, hid)], w_sem.at[1]),
        pltpu.make_async_copy(gout_hbm, gout_v, gout_sem),
    ]
    for q in range(cols):
        part = pl.ds(q * share * per_block, share * per_block)
        local.append(pltpu.make_async_copy(adj_hbm.at[part], adj_v.at[part], adj_sem.at[q]))
    local[0].start()

    barrier = pltpu.get_barrier_semaphore()

    def hello(d, _):
        pl.semaphore_signal(barrier, inc=1, device_id={"rows": lax.rem(me + d, parts)}, device_id_type=MESH)
        return 0

    lax.fori_loop(1, parts, hello, 0)
    for d in range(1, cols):
        pl.semaphore_signal(barrier, inc=1, device_id={"cols": lax.rem(mc + d, cols)}, device_id_type=MESH)
    pl.semaphore_wait(barrier, parts - 1 + cols - 1)

    def ask(d, _):
        p = lax.rem(me + d, parts)
        remote(fetch_ref, idx_v.at[me], idx_send.at[p], idx_recv.at[me], "rows", p).start()
        return 0

    lax.fori_loop(1, parts, ask, 0)
    idx_v[me] = jnp.full(idx_v.shape[1:], -1, jnp.int32)
    local[0].wait()

    def asked(d, _):
        p = lax.rem(me + parts - d, parts)
        remote(fetch_ref, idx_v.at[p], idx_send.at[p], idx_recv.at[p], "rows", p).wait_recv()
        return 0

    lax.fori_loop(1, parts, asked, 0)
    to_smem = pltpu.make_async_copy(idx_v, idx_s, smem_sem)
    to_smem.start()
    to_smem.wait()
    for offset in send_order(parts):
        p = at_offset(me, parts, offset)
        for s in range(cap):
            stage[p, s] = own_v[jnp.maximum(idx_s[p, s, me], 0)]
        remote(stage.at[p], pool.at[pl.ds(blocks + me * cap, cap)], tile_send.at[p], tile_recv.at[me], "rows", p).start()

    for d in range(1, cols):
        p = lax.rem(mc + d, cols)
        remote(own_v.at[pl.ds(p * share, share)], frows.at[mc], f_send.at[p], f_recv.at[mc], "cols", p).start()
    for copy in local[1:]:
        copy.start()

    def want(p, _):
        for s in range(cap):
            wanted_ref[p * cap + s] = idx_s[p, s, me]
        return 0

    lax.fori_loop(0, parts, want, 0)

    refs = blocks * per_block
    grid = (per_block, refs)
    place = lax.broadcasted_iota(jnp.int32, grid, 1)
    slots = jnp.zeros(grid, jnp.int32)
    table = slots_ref[...]
    for b in range(blocks):
        slots = jnp.where(place // per_block == b, table[:, b:b + 1], slots)
    slots = jnp.where(lax.rem(place, per_block) == lax.broadcasted_iota(jnp.int32, grid, 0), slots, 0)
    key_row = jnp.sum(slots, axis=0, keepdims=True) * refs + lax.broadcasted_iota(jnp.int32, (1, refs), 1)
    down = lax.broadcasted_iota(jnp.int32, (refs, refs), 0)
    across = lax.broadcasted_iota(jnp.int32, (refs, refs), 1)
    key_col = jnp.sum(jnp.where(down == across, key_row, 0), axis=1, keepdims=True)
    rank_col = jnp.sum(jnp.where(key_row < key_col, 1, 0), axis=1, keepdims=True)
    sort_v[0:1, :] = jnp.sum(jnp.where(rank_col == across, down, 0), axis=0, keepdims=True)
    before = jnp.where(key_col < (across + 1) * refs, 1, 0)
    sort_v[1:2, :] = jnp.sum(before, axis=0, keepdims=True) - 1
    sort_v[2:3, :] = jnp.sum(jnp.where(key_col < across * refs, 0, before), axis=0, keepdims=True)
    to_sort = pltpu.make_async_copy(sort_v, sort_s, sort_sem)
    to_sort.start()
    to_sort.wait()

    pool[pl.ds(blocks + me * cap, cap)] = jnp.zeros((cap,) + pool.shape[1:], BF16)
    for copy in local[1:]:
        copy.wait()
    for d in range(1, cols):
        p = lax.rem(mc + d, cols)
        remote(own_v.at[pl.ds(p * share, share)], frows.at[p], f_send.at[p], f_recv.at[p], "cols", p).wait()

    def given(d, _):
        p = lax.rem(me + parts - d, parts)
        remote(stage.at[p], pool.at[pl.ds(blocks + p * cap, cap)], tile_send.at[p], tile_recv.at[p], "rows", p).wait_recv()
        return 0

    lax.fori_loop(1, parts, given, 0)

    def aggregate(b):
        left = jnp.concatenate([adj_v[b * per_block + k] for k in range(per_block)], axis=1)
        right = jnp.concatenate([pool[colref_ref[k, b]] for k in range(per_block)], axis=0)
        return jnp.dot(left, right, preferred_element_type=F32).astype(BF16)

    def agg_copy(p, slot, i):
        return remote(agg_v.at[p, i], arows.at[slot, i], a_send.at[p, i], a_recv.at[slot, i], "cols", p)

    def back_copy(p, slot, g):
        part = pl.ds(g * step, step)
        return remote(gagg_v.at[p, part], gagg_in.at[slot, part], g_send.at[p, g], g_recv.at[slot, g], "cols", p)

    def tile_round(i):
        def one(d, _):
            p = lax.rem(mc + d, cols)
            agg_v[p, i] = aggregate(p * share + i)
            agg_copy(p, mc, i).start()
            return 0

        lax.fori_loop(1, cols, one, 0)
        arows[mc, i] = aggregate(mc * share + i)

    def dense(g):
        part = pl.ds(g * step, step)
        for j in range(step):
            for d in range(1, cols):
                p = lax.rem(mc + d, cols)
                agg_copy(p, p, g * step + j).wait_recv()

        def rows_of(ref):
            return jnp.concatenate([ref[c, part].reshape(step * tile, width) for c in range(cols)], axis=1)

        both = jnp.concatenate([rows_of(frows), rows_of(arows)], axis=1)
        v = jnp.dot(both, w_v[...], preferred_element_type=F32)
        c0 = math.sqrt(2.0 / math.pi)
        v2 = v * v
        t = jnp.tanh(c0 * v * (1.0 + 0.044715 * v2))
        half = 0.5 * (1.0 + t)
        act_v[part] = (v * half).astype(BF16).reshape(step, tile, hid)
        slope = half + (0.5 * v) * (1.0 - t * t) * (c0 * (1.0 + 3.0 * 0.044715 * v2))
        grad_pre = (gout_v[part].reshape(step * tile, hid).astype(F32) * slope).astype(BF16)
        nt = (((1,), (1,)), ((), ()))
        out = lax.dot_general(grad_pre, w_v[pl.ds(hid, hid)], nt, preferred_element_type=F32).astype(BF16)
        for c in range(cols):
            gagg_v[c, part] = out[:, c * width:(c + 1) * width].reshape(step, tile, width)
        for d in range(1, cols):
            back_copy(lax.rem(mc + d, cols), mc, g).start()
        gagg_in[mc, part] = gagg_v[mc, part]
        out = lax.dot_general(grad_pre, w_v[pl.ds(0, hid)], nt, preferred_element_type=F32).astype(BF16)
        for c in range(cols):
            self_v[c, part] = out[:, c * width:(c + 1) * width].reshape(step, tile, width)
        sums = lax.dot_general(both, grad_pre, (((0,), (0,)), ((), ())), preferred_element_type=F32)
        gw[...] += sums.reshape(gw.shape)

    def spread(g):
        for d in range(1, cols):
            p = lax.rem(mc + d, cols)
            back_copy(p, p, g).wait_recv()

        def one(n, _):
            c, i = n // step, g * step + lax.rem(n, step)
            at = (c * share + i) * per_block
            grad_t = gagg_in[c, i].T
            for k in range(0, per_block, 2):
                pair = jnp.concatenate([adj_v[at + k], adj_v[at + k + 1]], axis=1)
                out = jnp.dot(grad_t, pair, preferred_element_type=F32).astype(BF16)
                adj_v[at + k] = out[:, :tile]
                adj_v[at + k + 1] = out[:, tile:]
            return 0

        lax.fori_loop(0, cols * step, one, 0)

    gw[...] = jnp.zeros_like(gw)

    def work(g, _):
        @pl.when(g < groups)
        def _():
            for j in range(step):
                tile_round(g * step + j)

        @pl.when((g > 0) & (g <= groups))
        def _():
            dense(g - 1)

        @pl.when(g > 1)
        def _():
            spread(g - 2)

        return 0

    lax.fori_loop(0, groups + 1, work, 0)

    core = lax.rem(me, 2)
    mate = me + 1 - 2 * core
    pair = remote(gw.at[1 - core], from_core, core_send, core_recv, "rows", mate)
    pair.start()
    act_out = pltpu.make_async_copy(act_v, act_hbm, gout_sem)
    act_out.start()

    def share_copy(p, slot):
        return remote(stage.at[p], ret_hbm.at[slot], s_send.at[p], s_recv.at[slot], "rows", p)

    def self_copy(p, slot):
        return remote(self_v.at[p], selfp_hbm.at[slot], p_send.at[p], p_recv.at[slot], "cols", p)

    def others():
        return [lax.rem(mc + d, cols) for d in range(1, cols)]

    chips = parts // 2
    chip = me // 2

    def over_chips(f):
        def one(d, _):
            f(lax.rem(chip + d, chips))
            return 0

        lax.fori_loop(1, chips, one, 0)

    pair.wait()
    _, _, rows_p, cols_p = w_half.shape
    wide = hid // cols_p
    for c in range(cols):
        for q in range(chips):
            rows = pl.ds(c * (hid // cols) + (q // wide) * rows_p, rows_p)
            lanes = pl.ds((q % wide) * cols_p, cols_p)
            w_half[c, q] = gw[core, rows, lanes] + from_core[rows, lanes]
        w_out[c] = w_half[c].astype(BF16)

    def wz_copy(p, slot):
        return remote(w_out.at[p], w_in.at[slot], wz_send.at[p], wz_recv.at[slot], "cols", p)

    for p in others():
        wz_copy(p, mc).start()
    for p in others():
        self_copy(p, mc).start()
    own_self = pltpu.make_async_copy(self_v.at[mc], selfp_hbm.at[mc], own_sem)
    own_self.start()
    work(groups + 1, 0)

    def run(n, carry):
        last_slot, total = carry
        ref = sort_s[0, n]
        slot = colref_ref[lax.rem(ref, per_block), ref // per_block]
        total = jnp.where(slot == last_slot, total, 0.0) + adj_v[ref].astype(F32)
        run_v[n] = total.astype(BF16)
        return slot, total

    lax.fori_loop(0, refs, run, (jnp.int32(-1), jnp.zeros((width, tile), F32)), unroll=4)

    def drain_tiles(d, _):
        p = lax.rem(me + d, parts)
        remote(stage.at[p], pool.at[pl.ds(blocks + p * cap, cap)], tile_send.at[p], tile_recv.at[p], "rows", p).wait_send()
        return 0

    lax.fori_loop(1, parts, drain_tiles, 0)

    def share_of(slot):
        tile_sum = run_v[jnp.maximum(sort_s[1, slot], 0)]
        return jnp.where(sort_s[2, slot] > 0, tile_sum, jnp.zeros_like(tile_sum))

    order = send_order(parts)

    def shares(lo, hi):
        for offset in order[lo:hi]:
            p = at_offset(me, parts, offset)
            for n in range(cap):
                stage[p, n] = share_of(blocks + p * cap + n)
            share_copy(p, me).start()

    for p in others():
        wz_copy(p, p).wait()
    total = w_half[mc]
    for p in others():
        total = total + w_in[p].astype(F32)
    to_chip[...] = total.astype(BF16)

    def chip_copy(q, slot):
        return remote(to_chip.at[q], from_chip.at[slot], chip_send.at[q], chip_recv.at[slot], "rows", 2 * q + core)

    over_chips(lambda q: chip_copy(q, chip).start())
    shares(0, 7)
    from_chip[chip] = to_chip[chip]
    over_chips(lambda q: chip_copy(q, q).wait())
    total = from_chip[0].astype(F32)
    for q in range(1, chips):
        total = total + from_chip[q].astype(F32)
    sums[core, mc, chip] = total.astype(BF16)

    def up_copy(q, slot):
        return remote(sums.at[core, mc, chip], sums.at[core, mc, slot], up_send.at[q], up_recv.at[slot], "rows", 2 * q + core)

    over_chips(lambda q: up_copy(q, chip).start())
    shares(7, 14)
    over_chips(lambda q: up_copy(q, q).wait())

    def z_up(p, slot):
        return remote(sums.at[core, mc], sums.at[core, slot], z_send.at[p], z_recv.at[slot], "cols", p)

    for p in others():
        z_up(p, mc).start()
    shares(14, parts - 1)

    def own_share(t, _):
        pool[t] = share_of(t)
        return 0

    lax.fori_loop(0, blocks, own_share, 0)
    own_out = pltpu.make_async_copy(pool.at[pl.ds(0, blocks)], own_hbm, pool_sem)
    own_out.start()
    for p in others():
        z_up(p, p).wait()
    pair_up = remote(sums.at[core], sums.at[core], pair_send, pair_recv, "rows", mate)
    pair_up.start()
    pair_up.wait()
    sums_ref[...] = sums[...]

    for p in others():
        self_copy(p, p).wait()
    own_self.wait()
    own_out.wait()
    act_out.wait()

    def drain(d, _):
        p = lax.rem(me + d, parts)
        remote(fetch_ref, idx_v.at[p], idx_send.at[p], idx_recv.at[p], "rows", p).wait_send()
        share_copy(p, p).wait()
        return 0

    lax.fori_loop(1, parts, drain, 0)

    def drain_agg(i, _):
        for d in range(1, cols):
            p = lax.rem(mc + d, cols)
            agg_copy(p, p, i).wait_send()
        return 0

    lax.fori_loop(0, share, drain_agg, 0)

    def drain_back(g, _):
        for d in range(1, cols):
            p = lax.rem(mc + d, cols)
            back_copy(p, p, g).wait_send()
        return 0

    lax.fori_loop(0, groups, drain_back, 0)


def layer(fetch, colref, slots, feats, adj, w_self, w_neigh, gout, parts, cols, cap):
    refs, tile, _ = adj.shape
    blocks = feats.shape[0]
    per_block = refs // blocks
    width = feats.shape[-1]
    share = blocks // cols
    hid = cols * width
    step = 2
    groups = share // step
    chips = parts // 2
    piece = (16, 2 * hid * hid // (2 * cols * chips * 16))
    DMA = pltpu.SemaphoreType.DMA
    rows_shape = (cols, share, tile, width)
    return pl.pallas_call(
        functools.partial(layer_kernel, parts, cols, cap, blocks, per_block, step),
        out_shape=(
            jax.ShapeDtypeStruct(gout.shape, BF16),
            jax.ShapeDtypeStruct(rows_shape, BF16),
            jax.ShapeDtypeStruct((parts, cap, width, tile), BF16),
            jax.ShapeDtypeStruct((blocks, width, tile), BF16),
            jax.ShapeDtypeStruct((2, cols, chips) + piece, BF16),
            jax.ShapeDtypeStruct((parts * cap,), jnp.int32),
        ),
        in_specs=[VMEM, SMEM, VMEM, ANY, ANY, ANY, ANY, ANY],
        out_specs=(ANY, ANY, ANY, ANY, VMEM, SMEM),
        scratch_shapes=[
            pltpu.VMEM(gout.shape, BF16),
            pltpu.VMEM((blocks + parts * cap, tile, width), BF16),
            pltpu.VMEM(feats.shape, BF16),
            pltpu.VMEM(adj.shape, BF16),
            pltpu.VMEM((parts, cap, tile, width), BF16),
            pltpu.VMEM(rows_shape, BF16),
            pltpu.VMEM(rows_shape, BF16),
            pltpu.VMEM(rows_shape, BF16),
            pltpu.VMEM((2 * hid, hid), BF16),
            pltpu.VMEM(gout.shape, BF16),
            pltpu.VMEM(rows_shape, BF16),
            pltpu.VMEM(rows_shape, BF16),
            pltpu.VMEM(rows_shape, BF16),
            pltpu.VMEM((2, hid, hid), F32),
            pltpu.VMEM((hid, hid), F32),
            pltpu.VMEM((cols, chips) + piece, F32),
            pltpu.VMEM((cols, chips) + piece, BF16),
            pltpu.VMEM((cols, chips) + piece, BF16),
            pltpu.VMEM((chips,) + piece, BF16),
            pltpu.VMEM((chips,) + piece, BF16),
            pltpu.VMEM((2, cols, chips) + piece, BF16),
            pltpu.VMEM((refs, width, tile), BF16),
            pltpu.VMEM((8, refs), jnp.int32),
            pltpu.SMEM((8, refs), jnp.int32),
            pltpu.VMEM((parts,) + fetch.shape, jnp.int32),
            pltpu.SMEM((parts,) + fetch.shape, jnp.int32),
            DMA, DMA((cols,)), DMA, DMA, DMA((2,)), DMA, DMA, DMA,
            DMA((parts,)), DMA((parts,)), DMA((parts,)), DMA((parts,)),
            DMA((cols,)), DMA((cols,)), DMA((cols, share)), DMA((cols, share)),
            DMA((cols, groups)), DMA((cols, groups)), DMA, DMA,
            DMA((cols,)), DMA((cols,)), DMA((parts,)), DMA((parts,)), DMA((cols,)), DMA((cols,)),
            DMA((cols,)), DMA((cols,)), DMA((chips,)), DMA((chips,)), DMA((chips,)), DMA((chips,)), DMA, DMA,
        ],
        compiler_params=pltpu.CompilerParams(collective_id=0, has_side_effects=True, vmem_limit_bytes=63 << 20),
        name="layer",
    )(fetch, colref, slots, feats, adj, w_self, w_neigh, gout)


def combine_kernel(scale, wanted_ref, self_hbm, own_hbm, back_hbm, sums_hbm, act_hbm,
                   out_hbm, gs_hbm, gn_hbm, act_out_hbm,
                   self_v, own_v, back_v, sums_v, act_v, out_v, weights, total, in_sem, out_sem):
    moves = [
        pltpu.make_async_copy(src, dst, in_sem.at[n])
        for n, (src, dst) in enumerate(
            ((own_hbm, own_v), (back_hbm, back_v), (sums_hbm, sums_v), (self_hbm, self_v), (act_hbm, act_v))
        )
    ]
    for move in moves:
        move.start()
    moves[0].wait()
    total[...] = own_v[...].astype(F32)
    moves[1].wait()

    def add(s, _):
        t = wanted_ref[s]

        @pl.when(t >= 0)
        def _():
            total[t] += back_v[s].astype(F32)

        return 0

    lax.fori_loop(0, back_v.shape[0], add, 0)
    moves[2].wait()
    halves, cols, chips, rows_p, cols_p = sums_v.shape
    hid = weights.shape[1]
    wide = hid // cols_p
    for half in range(halves):
        for c in range(cols):
            for q in range(chips):
                at = c * (hid // cols) + (q // wide) * rows_p
                piece = sums_v[half, c, q].astype(F32) * scale
                weights[half, at:at + rows_p, (q % wide) * cols_p:(q % wide + 1) * cols_p] = piece
    done = [
        pltpu.make_async_copy(weights.at[half], ref, out_sem.at[half]) for half, ref in enumerate((gs_hbm, gn_hbm))
    ]
    moves[4].wait()
    done.append(pltpu.make_async_copy(act_v, act_out_hbm, out_sem.at[6]))
    for move in done:
        move.start()
    moves[3].wait()
    blocks = total.shape[0]
    chunks = 4
    size = blocks // chunks
    for n in range(chunks):
        def put(t, _):
            out_v[t] = self_v[t].astype(F32) + total[t].T
            return 0

        lax.fori_loop(n * size, (n + 1) * size, put, 0, unroll=4)
        part = pl.ds(n * size, size)
        done.append(pltpu.make_async_copy(out_v.at[part], out_hbm.at[part], out_sem.at[halves + n]))
        done[-1].start()
    for move in done:
        move.wait()


def combine(wanted, self_part, own, back, sums, act, scale):
    hid = self_part.shape[-1] * sums.shape[1]
    weights = jax.ShapeDtypeStruct((hid, hid), F32)
    return pl.pallas_call(
        functools.partial(combine_kernel, scale),
        out_shape=(jax.ShapeDtypeStruct(self_part.shape, F32), weights, weights, jax.ShapeDtypeStruct(act.shape, BF16)),
        in_specs=[SMEM, ANY, ANY, ANY, ANY, ANY],
        out_specs=(ANY, ANY, ANY, ANY),
        scratch_shapes=[
            pltpu.VMEM(self_part.shape, BF16),
            pltpu.VMEM(own.shape, BF16),
            pltpu.VMEM(back.shape, BF16),
            pltpu.VMEM(sums.shape, BF16),
            pltpu.VMEM(act.shape, BF16),
            pltpu.VMEM(self_part.shape, F32),
            pltpu.VMEM((2, hid, hid), F32),
            pltpu.VMEM(own.shape, F32),
            pltpu.SemaphoreType.DMA((5,)),
            pltpu.SemaphoreType.DMA((7,)),
        ],
        compiler_params=pltpu.CompilerParams(vmem_limit_bytes=62 << 20),
        name="combine",
    )(wanted, self_part, own, back, sums, act)


def body(feats, adj_vals, colref, fetch_ids, w_self, w_neigh, grad_out):
    node_rows, width = feats.shape
    blocks, per_block, tile, _ = adj_vals.shape
    parts = lax.axis_size("rows")
    cols = lax.axis_size("cols")
    cap = fetch_ids.shape[2]
    refs = blocks * per_block
    hid = width * cols
    scale = 1.0 / math.sqrt(node_rows * parts)
    fetch = jnp.pad(fetch_ids.reshape(parts, cap).T, ((0, 0), (0, 128 - parts)))
    gout = grad_out.reshape(blocks // cols, tile, hid)
    act, self_part, returned, own, sums, wanted = layer(
        fetch, colref.T, colref.T, feats.reshape(blocks, tile, width),
        adj_vals.reshape(refs, tile, tile), w_self, w_neigh, gout, parts, cols, cap,
    )
    grad_feats, grad_self, grad_neigh, act = combine(
        wanted, self_part.reshape(blocks, tile, width), own, returned.reshape(parts * cap, width, tile), sums, act, scale
    )
    return act.reshape(grad_out.shape), grad_self, grad_neigh, grad_feats.reshape(node_rows, width)


def solution(mesh):
    in_specs = (
        P("rows", "cols"),
        P("rows", None, None, None),
        P("rows", None),
        P("rows", None, None),
        P(),
        P(),
        P(("rows", "cols"), None),
    )
    out_specs = (P(("rows", "cols"), None), P(), P(), P("rows", "cols"))
    return jax.shard_map(body, mesh=mesh, in_specs=in_specs, out_specs=out_specs, check_vma=False)
```
